256 devices in a mesh: gx: 4 (over y), gy: 32 (over x, z), layer: 2 (over core).
Axes of the slice: x: 4, y: 4, z: 8, core: 2. Of those that a mesh axis runs over, the one named last changes fastest.
Arguments:
- profiles: bfloat16 [2, 4, 524288, 256], P('layer', 'gx', 'gy'), may hold values from 0.049804688 to 2
- time_weight: bfloat16 [256], replicated, may hold values from 0 to 0.029907227
- slot_cell: int32 [2, 4, 524288], P('layer', 'gx', 'gy'), may hold values from 0 to 65535
- inst_count: int32 [2, 4, 32], P('layer', 'gx', 'gy'), may hold values from 1 to 16384, as said below
- metal: float32 [6, 512, 16384], P('layer', 'gx', 'gy'), may hold values from 0.5 to 4
- via_density: float32 [512, 16384], P('gx', 'gy'), may hold values from 0.5 to 4
- pad: float32 [512, 16384], P('gx', 'gy'), may hold values from 0.05 to 0.5
- start_drop: float32 [6, 512, 16384], P('layer', 'gx', 'gy'), may hold values from 0 to 1
Outputs:
- drop: float32 [6, 512, 16384], P('layer', 'gx', 'gy')
- residual: float32 [6, 512, 16384], P('layer', 'gx', 'gy')
The draws below stay inside these ranges and needn't reach their ends.
Inputs may be any that keep to these rules, and one draw needn't show every extreme that they name: The first inst_count slots of a device are live, the rest are padding; and one device is full in every draw. `slot_cell`: row-major cell index within the tile of 128 x 512 cells.
All inputs are finite; a program needn't handle non-finite values.
Results may differ from the reference program's by a relative error of at most 0.0018.
Values sent between devices are 32-bit elements; how exact they have to be, the bound alone decides.
No kernel may reach another device: no remote copies, remote signals or barrier semaphores. Data moves between devices by JAX's collectives and lax.ppermute only.
A program may use at most 64 MiB of HBM per device.

```python
import math
import jax
import jax.numpy as jnp

CX = 128
CY = 512
INST_DEV = 16384
TIME = 256
ITERS = 3
GROUPS = 2
TILES_X = 4
TILES_Y = 32
NL = 6
NX = 512
NY = 16384


def draw_inst_count(key, part):
    key_factor, key_group, key_column = jax.random.split(jax.random.fold_in(key, 17), 3)
    tile_rows = jnp.arange(TILES_Y, dtype=jnp.int32)
    base_count = INST_DEV * (TILES_Y - 1 + 5 * tile_rows) // (6 * (TILES_Y - 1))
    factor = jax.random.randint(key_factor, (GROUPS, TILES_X, TILES_Y), 70, 101)
    counts = jnp.maximum(base_count[None, None, :] * factor // 100, 1)
    group_pick = jax.random.randint(key_group, (), 0, GROUPS)
    column_pick = jax.random.randint(key_column, (), 0, TILES_X)
    counts = counts.at[group_pick, column_pick, TILES_Y - 1].set(INST_DEV)
    return counts.astype(jnp.int32)


def with_ends(values, rng, low, top_value):
    longest = values.shape.index(max(values.shape))
    spots = []
    for shift in (0, 1):
        where = [jax.random.randint(jax.random.fold_in(rng, axis), (), 0, length) for axis, length in enumerate(values.shape)]
        where[longest] = (where[longest] + shift) % values.shape[longest]
        spots.append(tuple(where))
    return values.at[spots[0]].set(low).at[spots[1]].set(top_value)


def steps_of(key, shape, cuts, least, largest):
    gain, own = 1.0, jax.random.fold_in(key, 6)
    for axis_at, parts in cuts:
        draws = jnp.exp(jax.random.uniform(jax.random.fold_in(own, axis_at), (parts,), jnp.float32, least / len(cuts), largest / len(cuts)))
        gain = gain * jnp.repeat(draws, shape[axis_at] // parts).reshape([-1 if axis == axis_at else 1 for axis in range(len(shape))])
    return gain


def setup_inputs(seed: int = 0) -> dict:
    streams_of = jax.random.split(jax.random.key(seed), 9)
    return {
        "profiles": jnp.clip(jnp.exp(math.log(2.0) - 3.6927934 * jax.random.uniform(streams_of[0], (GROUPS, TILES_X, TILES_Y * INST_DEV, TIME), jnp.float32) ** steps_of(streams_of[0], (GROUPS, TILES_X, TILES_Y * INST_DEV, TIME), ((0, 2), (1, 4), (2, 32)), -0.2, 0.2)), 0.049804688, 2.0).astype(jnp.bfloat16),
        "time_weight": jnp.clip(jax.random.uniform(streams_of[1], (TIME,), jnp.float32, 0.0, 0.029907227), 0.0, 0.029907227).astype(jnp.bfloat16),
        "slot_cell": with_ends(jax.random.randint(streams_of[2], (GROUPS, TILES_X, TILES_Y * INST_DEV), 0, CX * CY), jax.random.fold_in(streams_of[2], 1), 0, (CX * CY) - 1).astype(jnp.int32),
        "inst_count": draw_inst_count(jax.random.fold_in(streams_of[8], 71), 0),
        "metal": jnp.clip(jnp.exp(math.log(4.0) - 2.0794415 * jax.random.uniform(streams_of[4], (NL, NX, NY), jnp.float32) ** steps_of(streams_of[4], (NL, NX, NY), ((0, 2), (1, 4), (2, 32)), -0.2, 0.2)), 0.5, 4.0),
        "via_density": jnp.clip(jnp.exp(math.log(4.0) - 2.0794415 * jax.random.uniform(streams_of[5], (NX, NY), jnp.float32) ** steps_of(streams_of[5], (NX, NY), ((0, 4), (1, 32)), -0.2, 0.2)), 0.5, 4.0),
        "pad": jnp.clip(jnp.exp(math.log(0.5) - 2.3025851 * jax.random.uniform(streams_of[6], (NX, NY), jnp.float32) ** steps_of(streams_of[6], (NX, NY), ((0, 4), (1, 32)), -0.2, 0.2)), 0.05, 0.5),
        "start_drop": jnp.clip(1.0 * jax.random.uniform(streams_of[7], (NL, NX, NY), jnp.float32) ** steps_of(streams_of[7], (NL, NX, NY), ((0, 2), (1, 4), (2, 32)), -0.2, 0.2), 0.0, 1.0),
    }


def harmonic(values, beside):
    return 2.0 * values * beside / (values + beside)


def links(extended, via_column):
    middle = extended[1:-1, 1:-1, 1:-1]
    east_link = harmonic(middle, extended[1:-1, 2:, 1:-1])
    west_link = harmonic(middle, extended[1:-1, :-2, 1:-1])
    north_link = harmonic(middle, extended[1:-1, 1:-1, 2:])
    south_link = harmonic(middle, extended[1:-1, 1:-1, :-2])
    upper_link = via_column * harmonic(middle, extended[2:, 1:-1, 1:-1])
    lower_link = via_column * harmonic(middle, extended[:-2, 1:-1, 1:-1])
    return (east_link, west_link, north_link, south_link, upper_link, lower_link)


def diagonal_of(conduct):
    east_link, west_link, north_link, south_link, upper_link, lower_link = conduct
    return east_link + west_link + north_link + south_link + upper_link + lower_link


def operate(field, extended, conduct, diagonal):
    east_link, west_link, north_link, south_link, upper_link, lower_link = conduct
    result = diagonal * field - east_link * extended[1:-1, 2:, 1:-1] - west_link * extended[1:-1, :-2, 1:-1]
    result = result - north_link * extended[1:-1, 1:-1, 2:] - south_link * extended[1:-1, 1:-1, :-2]
    return result - upper_link * extended[2:, 1:-1, 1:-1] - lower_link * extended[:-2, 1:-1, 1:-1]


def reference(profiles, time_weight, slot_cell, inst_count, metal, via_density, pad, start_drop):
    slot_current = jnp.dot(profiles.reshape(-1, TIME), time_weight, preferred_element_type=jnp.float32)
    slot_current = slot_current.reshape(GROUPS, TILES_X, TILES_Y, INST_DEV)
    positions = jnp.arange(INST_DEV, dtype=jnp.int32)
    slot_current = jnp.where(positions[None, None, None, :] < inst_count[..., None], slot_current, 0.0)
    cells = slot_cell.reshape(GROUPS, TILES_X, TILES_Y, INST_DEV)
    row_base = (jnp.arange(TILES_X, dtype=jnp.int32) * CX)[None, :, None, None]
    col_base = (jnp.arange(TILES_Y, dtype=jnp.int32) * CY)[None, None, :, None]
    flat_index = ((cells // CY + row_base) * NY + cells % CY + col_base).reshape(-1).astype(jnp.int32)
    current = jax.ops.segment_sum(slot_current.reshape(-1), flat_index, num_segments=NX * NY).reshape(NX, NY)
    rhs = jnp.zeros_like(metal).at[0].set(current.astype(metal.dtype))
    conduct = links(jnp.pad(metal, 1), via_density[None])
    diagonal = diagonal_of(conduct).at[-1].add(pad)

    def apply(field):
        return operate(field, jnp.pad(field, 1), conduct, diagonal)

    solution = start_drop
    residual = rhs - apply(start_drop)
    scaled = residual / diagonal
    direction = scaled
    energy = jnp.sum(residual * scaled)
    for iteration in range(ITERS):
        image = apply(direction)
        step_size = energy / jnp.sum(direction * image)
        solution = solution + step_size * direction
        residual = residual - step_size * image
        if iteration + 1 < ITERS:
            scaled = residual / diagonal
            energy_next = jnp.sum(residual * scaled)
            direction = scaled + (energy_next / energy) * direction
            energy = energy_next
    return solution, residual
```

```python
import jax
import jax.numpy as jnp
from jax import lax
from jax.experimental import pallas as pl
from jax.experimental.pallas import tpu as pltpu
from jax.sharding import Mesh
from jax.sharding import PartitionSpec as P

ALL = ("gx", "gy_0", "gy_1", "layer")
GY = ("gy_0", "gy_1")
HALO = 4
LANES = 128
SIDE = 256
SLOTS = 2048
CHUNK = 512
TINY = 1e-30
MOMENTS = 6

VMEM = pl.BlockSpec(memory_space=pltpu.VMEM)
SMEM = pl.BlockSpec(memory_space=pltpu.SMEM)


def params(mebibytes):
    return pltpu.CompilerParams(vmem_limit_bytes=mebibytes << 20)


def scatter_kernel(count_ref, weight_ref, profile_ref, cell_ref, out_ref, total_ref):
    step = pl.program_id(0)

    @pl.when(step == 0)
    def _():
        total_ref[...] = jnp.zeros_like(total_ref)

    @pl.when(step * SLOTS < count_ref[0])
    def _():
        half = out_ref.shape[0]
        for first in range(0, SLOTS, CHUNK):
            amount = lax.dot_general(
                weight_ref[...],
                profile_ref[first : first + CHUNK, :],
                (((1,), (1,)), ((), ())),
                preferred_element_type=jnp.float32,
            )[:1]
            position = step * SLOTS + first + lax.broadcasted_iota(jnp.int32, (1, CHUNK), 1)
            amount = jnp.where(position < count_ref[0], amount, 0.0)
            high = amount.astype(jnp.bfloat16).astype(jnp.float32)
            low = amount - high
            cell = cell_ref[:, first : first + CHUNK]
            row = (cell >> 9) + ((cell >> 8) & 1) * half
            col = cell & (SIDE - 1)
            ids = lax.broadcasted_iota(jnp.int32, (SIDE, CHUNK), 0)
            here = ids == row
            left = jnp.concatenate(
                [
                    jnp.where(here, high, 0.0).astype(jnp.bfloat16),
                    jnp.where(here, low, 0.0).astype(jnp.bfloat16),
                ],
                axis=0,
            )
            right = jnp.where(ids == col, 1.0, 0.0).astype(jnp.bfloat16)
            total_ref[...] += lax.dot_general(
                left, right, (((1,), (1,)), ((), ())), preferred_element_type=jnp.float32
            )

    @pl.when(step == pl.num_programs(0) - 1)
    def _():
        half = out_ref.shape[0]
        both = total_ref[:SIDE, :] + total_ref[SIDE:, :]
        out_ref[:, :SIDE] = both[:half]
        out_ref[:, SIDE:] = both[half:]


def scatter(profiles, time_weight, slot_cell, inst_count, tile):
    slots, times = profiles.shape[-2:]
    return pl.pallas_call(
        scatter_kernel,
        out_shape=jax.ShapeDtypeStruct(tile, jnp.float32),
        grid=(slots // SLOTS,),
        in_specs=[
            SMEM,
            pl.BlockSpec((16, times), lambda i: (0, 0)),
            pl.BlockSpec((SLOTS, times), lambda i: (i, 0)),
            pl.BlockSpec((1, SLOTS), lambda i: (0, i)),
        ],
        out_specs=pl.BlockSpec(tile, lambda i: (0, 0)),
        scratch_shapes=[pltpu.VMEM((2 * SIDE, SIDE), jnp.float32)],
        compiler_params=params(24),
        cost_estimate=pl.CostEstimate(
            flops=6 * slots * SIDE * SIDE, bytes_accessed=2 * slots * times, transcendentals=0
        ),
        name="scatter",
    )(
        inst_count.reshape(1),
        jnp.broadcast_to(time_weight[None], (16, times)),
        profiles.reshape(slots, times),
        slot_cell.reshape(1, slots),
    )


def plane_readers(metal, other_metal, start, other_start, via, pad, mine, theirs, flip):
    readers = []
    for own, other in ((metal, other_metal), (start, other_start)):
        for ref in (own, other):
            for k in range(3):
                index = jnp.where(flip == 1, 2 - k, k)
                readers.append(lambda rows, cols, ref=ref, index=index: ref[index, rows, cols])
    readers.append(lambda rows, cols: via[rows, cols])
    readers.append(lambda rows, cols: pad[rows, cols])
    readers.append(lambda rows, cols: mine[rows, cols] + theirs[rows, cols])
    return readers


def rows_kernel(flag, m, om, s, os, via, pad, mine, theirs, first_ref, last_ref):
    rows = m.shape[1]
    readers = plane_readers(m, om, s, os, via, pad, mine, theirs, flag[0])
    low = lax.broadcasted_iota(jnp.int32, (8, m.shape[2]), 0) < HALO
    for ref, start in ((first_ref, 0), (last_ref, rows - 8)):
        span = slice(start, start + 8)
        for pair in range(0, len(readers), 2):
            one = readers[pair](span, slice(None))
            two = one
            if pair + 1 < len(readers):
                two = pltpu.roll(readers[pair + 1](span, slice(None)), HALO, 0)
            packed = jnp.where(low, one, two) if start == 0 else jnp.where(low, two, one)
            ref[pair * HALO : pair * HALO + 8, :] = packed


def row_halo(after, before, plane, cols, flag):
    span = slice(plane // 2 * 8, plane // 2 * 8 + 8)
    tail = jnp.where(flag[2] == 1, after[span, cols], 0.0)
    head = jnp.where(flag[1] == 1, before[span, cols], 0.0)
    low = lax.broadcasted_iota(jnp.int32, tail.shape, 0) < HALO
    if plane % 2 == 0:
        return jnp.where(low, tail, head)
    return pltpu.roll(jnp.where(low, head, tail), HALO, 0)


def cols_kernel(flag, m, om, s, os, via, pad, mine, theirs, after, before, first_ref, last_ref):
    rows, cols = m.shape[1], m.shape[2]
    readers = plane_readers(m, om, s, os, via, pad, mine, theirs, flag[0])
    for ref, start in ((first_ref, 0), (last_ref, cols - LANES)):
        span = slice(start, start + LANES)
        lane = lax.broadcasted_iota(jnp.int32, (rows + 8, LANES), 1)
        packed = jnp.zeros((rows + 8, LANES), jnp.float32)
        for plane, read in enumerate(readers):
            values = jnp.concatenate(
                [read(slice(None), span), row_halo(after, before, plane, span, flag)], axis=0
            )
            where = HALO * plane if start == 0 else (LANES - HALO + HALO * plane) % LANES
            turned = pltpu.roll(values, HALO * plane, 1) if plane else values
            packed = jnp.where((lane >= where) & (lane < where + HALO), turned, packed)
        ref[...] = packed


def col_halo(right, left, plane, flag):
    lane = lax.broadcasted_iota(jnp.int32, right.shape, 1)
    where = HALO * plane
    back = (LANES - HALO + where) % LANES
    tail = (lane >= where) & (lane < where + HALO) & (flag[4] == 1)
    head = (lane >= back) & (lane < back + HALO) & (flag[3] == 1)
    values = jnp.where(tail, right[...], jnp.where(head, left[...], 0.0))
    return pltpu.roll(values, (LANES - where) % LANES, 1) if plane else values


def strip_call(kernel, shape, name, *operands):
    return pl.pallas_call(
        kernel,
        out_shape=(jax.ShapeDtypeStruct(shape, jnp.float32),) * 2,
        in_specs=[SMEM] + [VMEM] * (len(operands) - 1),
        out_specs=(VMEM, VMEM),
        compiler_params=params(24),
        name=name,
    )(*operands)


def after_row(values):
    return pltpu.roll(values, values.shape[0] - 1, 0)


def before_row(values):
    return pltpu.roll(values, 1, 0)


def after_col(values):
    return pltpu.roll(values, values.shape[1] - 1, 1)


def before_col(values):
    return pltpu.roll(values, 1, 1)


def harmonic(values, beside):
    return 2.0 * values * beside / jnp.maximum(values + beside, TINY)


def basis_kernel(
    flag, m, om, s, os, via, pad, mine, theirs, after, before, right, left,
    diag_out, z0_out, z1_out, z2_out, w2_out, moments_ref,
    metal_ref, start_ref, column_ref, row_link, col_link, up_link, diag_ref, inv_ref, r_ref, z_ref, v_ref,
):
    rows, cols = m.shape[1], m.shape[2]
    flip = flag[0]
    readers = plane_readers(m, om, s, os, via, pad, mine, theirs, flip)
    places = [metal_ref.at[k] for k in range(6)] + [start_ref.at[k] for k in range(6)]
    places += [column_ref.at[k] for k in range(3)]
    every = slice(None)
    for plane, (read, place) in enumerate(zip(readers, places)):
        place[:rows, :cols] = read(every, every)
        place[rows:, :cols] = row_halo(after, before, plane, every, flag)
        place[:, cols:] = col_halo(right, left, plane, flag)

    up_link[0] = jnp.zeros_like(up_link[0])
    up_link[6] = jnp.zeros_like(up_link[0])

    def link(k, _):
        metal = metal_ref[k]
        row_link[k] = harmonic(metal, after_row(metal))
        col_link[k] = harmonic(metal, after_col(metal))
        return 0

    lax.fori_loop(0, 6, link, 0)

    def climb(k, _):
        up_link[k + 1] = column_ref[0] * harmonic(metal_ref[k], metal_ref[k + 1])
        return 0

    lax.fori_loop(0, 5, climb, 0)

    padded_layer = jnp.where(flip == 1, 0, 5)
    fed_layer = 5 - padded_layer

    def operate(field, k):
        v = field[k]
        row, col = row_link[k], col_link[k]
        result = diag_ref[k] * v - row * after_row(v) - before_row(row * v)
        result = result - col * after_col(v) - before_col(col * v)
        above, below = jnp.minimum(k + 1, 5), jnp.maximum(k - 1, 0)
        return result - up_link[k + 1] * field[above] - up_link[k] * field[below]

    def diagonal(k, _):
        row, col = row_link[k], col_link[k]
        total = row + before_row(row) + col + before_col(col) + up_link[k + 1] + up_link[k]
        total = total + jnp.where(k == padded_layer, column_ref[1], 0.0)
        diag_ref[k] = total
        inv_ref[k] = 1.0 / jnp.maximum(total, TINY)
        return 0

    lax.fori_loop(0, 6, diagonal, 0)

    def own(values):
        return values[:rows, :cols]

    def first(k, _):
        r = jnp.where(k == fed_layer, column_ref[2], 0.0) - operate(start_ref, k)
        r_ref[k] = r
        z_ref[k] = r * inv_ref[k]
        return 0

    lax.fori_loop(0, 6, first, 0)

    def second(k, _):
        r = r_ref[k] - operate(z_ref, k)
        v_ref[k] = r * inv_ref[k]
        return 0

    lax.fori_loop(0, 5, second, 0)

    def keep(k, sums):
        z0, z1, r0 = own(z_ref[k]), own(v_ref[k]), own(r_ref[k])
        z0_out[k] = z0
        z1_out[k] = z1
        diag_out[k] = own(diag_ref[k])
        return sums[0] + fold(z0 * r0), sums[1] + fold(z1 * r0)

    def fold(values):
        return values.reshape(rows // 8, 8, cols // LANES, LANES).sum(axis=(0, 2))

    zero = jnp.zeros((8, LANES), jnp.float32)
    sums = lax.fori_loop(0, 3, keep, (zero, zero))

    def third(k, sums):
        r = diag_ref[k] * v_ref[k] - operate(v_ref, k)
        z_ref[k] = r * inv_ref[k]
        return 0

    lax.fori_loop(0, 4, third, 0)

    def fourth(k, sums):
        z1, z2, d = own(v_ref[k]), own(z_ref[k]), own(diag_ref[k])
        w2 = own(operate(z_ref, k))
        z2_out[k] = z2
        w2_out[k] = w2
        d2 = d * z2
        terms = (d * z1 * z1, z1 * d2, z2 * d2, z2 * (d2 - w2))
        return tuple(total + fold(term) for total, term in zip(sums, terms))

    sums = sums + lax.fori_loop(0, 3, fourth, (zero,) * 4)
    lane = lax.broadcasted_iota(jnp.int32, (8, LANES), 1)
    packed = zero
    for k, total in enumerate(sums):
        packed = jnp.where(lane == k, jnp.sum(total, keepdims=True), packed)
    moments_ref[...] = jnp.broadcast_to(packed[:1], moments_ref.shape)


def basis(devices, *operands):
    own = operands[1].shape
    full = (own[1] + 8, own[2] + LANES)
    layers = pltpu.VMEM((6,) + full, jnp.float32)
    return pl.pallas_call(
        basis_kernel,
        out_shape=(jax.ShapeDtypeStruct(own, jnp.float32),) * 5
        + (jax.ShapeDtypeStruct((devices, LANES), jnp.float32),),
        in_specs=[SMEM] + [VMEM] * (len(operands) - 1),
        out_specs=(VMEM,) * 6,
        scratch_shapes=[
            layers,
            layers,
            pltpu.VMEM((3,) + full, jnp.float32),
            layers,
            layers,
            pltpu.VMEM((7,) + full, jnp.float32),
            layers,
            layers,
            layers,
            layers,
            layers,
        ],
        compiler_params=params(50),
        name="basis",
    )(*operands)


def product(one, two, moments):
    total = 0.0
    for i, a in enumerate(one):
        for j, b in enumerate(two):
            total = total + a * b * moments[i + j]
    return total


def coefficients(moments, iterations):
    drops = [moments[i] - moments[i + 1] for i in range(MOMENTS - 1)]
    one = jnp.ones_like(moments[0])
    residual, direction, iterate = [one], [one], [0.0 * one] * iterations
    energy = moments[0]
    for iteration in range(iterations):
        step = energy / product(direction, direction, drops)
        iterate = [x + step * (direction[i] if i < len(direction) else 0.0) for i, x in enumerate(iterate)]
        image = [a - b for a, b in zip(direction + [0.0], [0.0] + direction)]
        residual = [a - step * b for a, b in zip(residual + [0.0], image)]
        if iteration + 1 < iterations:
            after = product(residual, residual, moments)
            ratio = after / energy
            direction = [a + ratio * b for a, b in zip(residual, direction + [0.0])]
            energy = after
    return iterate, residual


def update_kernel(flag, sums, start, diag, z0_ref, z1_ref, z2_ref, w2_ref, drop_ref, residual_ref):
    sums = jnp.sum(sums[...], axis=0, keepdims=True)
    lane = lax.broadcasted_iota(jnp.int32, sums.shape, 1)
    moments = [
        jnp.sum(jnp.where(lane == k, sums, 0.0), axis=1, keepdims=True) for k in range(MOMENTS)
    ]
    x, r = coefficients(moments, 3)
    for k in range(3):
        index = jnp.where(flag[0] == 1, 2 - k, k)
        z0, z1, z2 = z0_ref[k], z1_ref[k], z2_ref[k]
        drop_ref[index] = start[index] + (x[0] * z0 + x[1] * z1 + x[2] * z2)
        inner = r[0] * z0 + r[1] * z1 + (r[2] + r[3]) * z2
        residual_ref[index] = diag[k] * inner - r[3] * w2_ref[k]


def update(*operands):
    shape = jax.ShapeDtypeStruct(operands[2].shape, jnp.float32)
    return pl.pallas_call(
        update_kernel,
        out_shape=(shape, shape),
        in_specs=[SMEM] + [VMEM] * (len(operands) - 1),
        out_specs=(VMEM, VMEM),
        compiler_params=params(24),
        name="update",
    )(*operands)


def ring(value, axes, shift):
    count = lax.axis_size(axes)
    return lax.ppermute(value, axes, [(i, (i + shift) % count) for i in range(count)])


def per_device(profiles, time_weight, slot_cell, inst_count, metal, via_density, pad, start_drop):
    rows, cols = metal.shape[1], metal.shape[2]
    gx, gy, layer = lax.axis_index("gx"), lax.axis_index(GY), lax.axis_index("layer")
    flag = jnp.stack(
        [
            layer,
            gx > 0,
            gx < lax.axis_size("gx") - 1,
            gy > 0,
            gy < lax.axis_size(GY) - 1,
        ]
    ).astype(jnp.int32)
    other_metal = ring(metal, "layer", 1)
    other_start = ring(start_drop, "layer", 1)
    mine = scatter(profiles, time_weight, slot_cell, inst_count, (rows, cols))
    theirs = ring(mine, "layer", 1)
    planes = (flag, metal, other_metal, start_drop, other_start, via_density, pad, mine, theirs)
    first, last = strip_call(rows_kernel, (64, cols), "rows", *planes)
    after, before = ring(first, "gx", -1), ring(last, "gx", 1)
    first, last = strip_call(cols_kernel, (rows + 8, LANES), "cols", *planes, after, before)
    right, left = ring(first, GY, -1), ring(last, GY, 1)
    devices = lax.axis_size(ALL)
    diag, z0, z1, z2, w2, moments = basis(devices, *planes, after, before, right, left)
    sums = lax.all_to_all(moments, ALL, 0, 0, tiled=True)
    return update(flag, sums, start_drop, diag, z0, z1, z2, w2)


def solution(mesh):
    split = Mesh(
        mesh.devices.reshape(mesh.shape["gx"], 4, 8, mesh.shape["layer"]),
        ("gx", "gy_0", "gy_1", "layer"),
    )
    grid = P("layer", "gx", GY)
    return jax.shard_map(
        per_device,
        mesh=split,
        in_specs=(P("layer", "gx", GY, None), P(), grid, grid, grid, P("gx", GY), P("gx", GY), grid),
        out_specs=(grid, grid),
        check_vma=False,
    )
```

```python
import jax
import jax.numpy as jnp
from jax import lax
from jax.experimental import pallas as pl
from jax.experimental.pallas import tpu as pltpu
from jax.sharding import Mesh
from jax.sharding import PartitionSpec as P

ALL = ("gx", "gy_0", "gy_1", "layer")
GY = ("gy_0", "gy_1")
HALO = 4
LANES = 128
SIDE = 256
CHUNK = 4096
TINY = 1e-30
MOMENTS = 6

VMEM = pl.BlockSpec(memory_space=pltpu.VMEM)
HBM = pl.BlockSpec(memory_space=pltpu.HBM)
SMEM = pl.BlockSpec(memory_space=pltpu.SMEM)


def params(mebibytes):
    return pltpu.CompilerParams(vmem_limit_bytes=mebibytes << 20)


def scatter_kernel(count_ref, weight_ref, profile_hbm, cell_hbm, out_ref, profile_ref, cell_ref, total_ref, sems):
    half = out_ref.shape[0]
    blocks = profile_ref.shape[0] // CHUNK
    fetches = [pltpu.make_async_copy(cell_hbm, cell_ref, sems.at[blocks])]
    for block in range(blocks):
        span = pl.ds(block * CHUNK, CHUNK)
        fetches.append(
            pltpu.make_async_copy(profile_hbm.at[span], profile_ref.at[span], sems.at[block])
        )
    for fetch in fetches:
        fetch.start()
    total_ref[...] = jnp.zeros_like(total_ref)
    weight = jnp.broadcast_to(weight_ref[...], (16, weight_ref.shape[1]))
    ids = lax.broadcasted_iota(jnp.int32, (SIDE, CHUNK), 0).astype(jnp.float32).astype(jnp.bfloat16)
    zero, one = jnp.bfloat16(0), jnp.bfloat16(1)
    fetches[0].wait()

    def add_block(block, _):
        first = pl.multiple_of(block * CHUNK, CHUNK)
        span = pl.ds(first, CHUNK)
        pltpu.make_async_copy(profile_hbm.at[span], profile_ref.at[span], sems.at[block]).wait()
        amount = lax.dot_general(
            weight,
            profile_ref[span, :],
            (((1,), (1,)), ((), ())),
            preferred_element_type=jnp.float32,
        )[:1]
        position = first + lax.broadcasted_iota(jnp.int32, (1, CHUNK), 1)
        amount = jnp.where(position < count_ref[0], amount, 0.0)
        high = amount.astype(jnp.bfloat16)
        low = (amount - high.astype(jnp.float32)).astype(jnp.bfloat16)
        cell = cell_ref[:, span]
        row = ((cell >> 9) + ((cell >> 8) & 1) * half).astype(jnp.float32).astype(jnp.bfloat16)
        col = (cell & (SIDE - 1)).astype(jnp.float32).astype(jnp.bfloat16)
        here = ids == row
        left = jnp.concatenate([jnp.where(here, high, zero), jnp.where(here, low, zero)], axis=0)
        right = jnp.where(ids == col, one, zero)
        total_ref[...] += lax.dot_general(
            left, right, (((1,), (1,)), ((), ())), preferred_element_type=jnp.float32
        )
        return 0

    lax.fori_loop(0, blocks, add_block, 0)
    both = total_ref[:SIDE, :] + total_ref[SIDE:, :]
    out_ref[:, :SIDE] = both[:half]
    out_ref[:, SIDE:] = both[half:]


def scatter(profiles, time_weight, slot_cell, inst_count, tile):
    slots, times = profiles.shape[-2:]
    return pl.pallas_call(
        scatter_kernel,
        out_shape=jax.ShapeDtypeStruct(tile, jnp.float32),
        in_specs=[SMEM, VMEM, HBM, HBM],
        out_specs=VMEM,
        scratch_shapes=[
            pltpu.VMEM((slots, times), jnp.bfloat16),
            pltpu.VMEM((1, slots), jnp.int32),
            pltpu.VMEM((2 * SIDE, SIDE), jnp.float32),
            pltpu.SemaphoreType.DMA((slots // CHUNK + 1,)),
        ],
        compiler_params=params(24),
        cost_estimate=pl.CostEstimate(
            flops=6 * slots * SIDE * SIDE, bytes_accessed=2 * slots * times, transcendentals=0
        ),
        name="scatter",
    )(
        inst_count.reshape(1),
        time_weight.reshape(1, times),
        pltpu.with_memory_space_constraint(profiles.reshape(slots, times), pltpu.HBM),
        pltpu.with_memory_space_constraint(slot_cell.reshape(1, slots), pltpu.HBM),
    )


def plane_readers(metal, other_metal, start, other_start, via, pad, mine, theirs, flip):
    readers = []
    for own, other in ((metal, other_metal), (start, other_start)):
        for ref in (own, other):
            for k in range(3):
                index = jnp.where(flip == 1, 2 - k, k)
                readers.append(lambda rows, cols, ref=ref, index=index: ref[index, rows, cols])
    readers.append(lambda rows, cols: via[rows, cols])
    readers.append(lambda rows, cols: pad[rows, cols])
    readers.append(lambda rows, cols: mine[rows, cols] + theirs[rows, cols])
    return readers


def rows_kernel(flag, m, om, s, os, via, pad, mine, theirs, first_ref, last_ref):
    rows = m.shape[1]
    readers = plane_readers(m, om, s, os, via, pad, mine, theirs, flag[0])
    low = lax.broadcasted_iota(jnp.int32, (8, m.shape[2]), 0) < HALO
    for ref, start in ((first_ref, 0), (last_ref, rows - 8)):
        span = slice(start, start + 8)
        for pair in range(0, len(readers), 2):
            one = readers[pair](span, slice(None))
            two = one
            if pair + 1 < len(readers):
                two = pltpu.roll(readers[pair + 1](span, slice(None)), HALO, 0)
            packed = jnp.where(low, one, two) if start == 0 else jnp.where(low, two, one)
            ref[pair * HALO : pair * HALO + 8, :] = packed


def row_halo(ref, plane, cols, inside):
    values = jnp.where(inside == 1, ref[plane // 2 * 8 : plane // 2 * 8 + 8, cols], 0.0)
    return pltpu.roll(values, HALO, 0) if plane % 2 else values


def cols_kernel(flag, m, om, s, os, via, pad, mine, theirs, after, before, first_ref, last_ref):
    rows, cols = m.shape[1], m.shape[2]
    readers = plane_readers(m, om, s, os, via, pad, mine, theirs, flag[0])
    for ref, start in ((first_ref, 0), (last_ref, cols - LANES)):
        span = slice(start, start + LANES)
        lane = lax.broadcasted_iota(jnp.int32, (rows + 16, LANES), 1)
        packed = jnp.zeros((rows + 16, LANES), jnp.float32)
        for plane, read in enumerate(readers):
            values = jnp.concatenate(
                [
                    row_halo(before, plane, span, flag[1]),
                    read(slice(None), span),
                    row_halo(after, plane, span, flag[2]),
                ],
                axis=0,
            )
            where = HALO * plane if start == 0 else (LANES - HALO + HALO * plane) % LANES
            turned = pltpu.roll(values, HALO * plane, 1) if plane else values
            packed = jnp.where((lane >= where) & (lane < where + HALO), turned, packed)
        ref[...] = packed


def col_halo(right, left, plane, flag):
    lane = lax.broadcasted_iota(jnp.int32, right.shape, 1)
    where = HALO * plane
    back = (LANES - HALO + where) % LANES
    tail = (lane >= where) & (lane < where + HALO) & (flag[4] == 1)
    head = (lane >= back) & (lane < back + HALO) & (flag[3] == 1)
    values = jnp.where(tail, right[...], jnp.where(head, left[...], 0.0))
    return pltpu.roll(values, (LANES - where) % LANES, 1) if plane else values


def strip_call(kernel, shape, name, *operands):
    return pl.pallas_call(
        kernel,
        out_shape=(jax.ShapeDtypeStruct(shape, jnp.float32),) * 2,
        in_specs=[SMEM] + [VMEM] * (len(operands) - 1),
        out_specs=(VMEM, VMEM),
        compiler_params=params(24),
        name=name,
    )(*operands)


OWN = 16


def harmonic(values, beside):
    return 2.0 * values * beside / jnp.maximum(values + beside, TINY)


def basis_kernel(
    flag, m, om, s, os, via, pad, mine, theirs, after, before, right, left,
    inv_out, r0_out, s1_out, s2_out, s3_out, moments_ref,
    metal_ref, start_ref, column_ref, row_link, col_link, up_link, inv_ref, z0_ref, z1_ref, z2_ref,
):
    rows, cols = m.shape[1], m.shape[2]
    tiles, strips = cols // LANES, rows // 8
    flip = flag[0]
    readers = plane_readers(m, om, s, os, via, pad, mine, theirs, flip)
    places = [(metal_ref, k) for k in range(6)] + [(start_ref, k) for k in range(6)]
    places += [(column_ref, k) for k in range(3)]
    for plane, (read, (ref, k)) in enumerate(zip(readers, places)):
        for j in range(tiles):
            span = slice(j * LANES, j * LANES + LANES)
            ref[k, j, OWN - 8 : OWN, :] = row_halo(before, plane, span, flag[1])
            ref[k, j, OWN : OWN + rows, :] = read(slice(None), span)
            ref[k, j, OWN + rows : OWN + rows + 8, :] = row_halo(after, plane, span, flag[2])
        ref[k, tiles, OWN - 8 : OWN + rows + 8, :] = col_halo(right, left, plane, flag)

    lane = lax.broadcasted_iota(jnp.int32, (tiles + 1, 8, LANES), 2)

    def after_col(values):
        turned = pltpu.roll(values, LANES - 1, 2)
        return jnp.where(lane == LANES - 1, jnp.concatenate([turned[1:], turned[:1]], 0), turned)

    def before_col(values):
        turned = pltpu.roll(values, 1, 2)
        return jnp.where(lane == 0, jnp.concatenate([turned[-1:], turned[:-1]], 0), turned)

    def put(ref, k, i, values):
        ref[k, :, pl.ds(OWN + 8 * i, 8), :] = values

    def put_own(ref, k, i, values):
        for j in range(tiles):
            ref[k, pl.ds(8 * i, 8), j * LANES : j * LANES + LANES] = values[j]

    def fold(values):
        return jnp.sum(values[:tiles], axis=0)

    def sweep(body, count):
        body(-1, None)
        zero = jnp.zeros((8, LANES), jnp.float32)
        sums = lax.fori_loop(0, strips, body, (zero,) * count)
        body(strips, None)
        return sums

    weight = jnp.where(flip == 1, 1.0, 0.0)

    def first(i, sums):
        def get(ref, k, off=0):
            return ref[k, :, pl.ds(OWN + 8 * i + off, 8), :]

        energy = None if sums is None else sums[0]
        up_before = None
        for k in range(6):
            metal, x = get(metal_ref, k), get(start_ref, k)
            row = harmonic(metal, get(metal_ref, k, 1))
            put(row_link, k, i, row)
            row_before = get(row_link, k, -1)
            col = harmonic(metal, after_col(metal))
            put(col_link, k, i, col)
            total = row + row_before + col + before_col(col)
            near = row * get(start_ref, k, 1) + row_before * get(start_ref, k, -1)
            near = near + col * after_col(x) + before_col(col * x)
            if k < 5:
                up = get(column_ref, 0) * harmonic(metal, get(metal_ref, k + 1))
                put(up_link, k, i, up)
                total = total + up
                near = near + up * get(start_ref, k + 1)
            if k > 0:
                total = total + up_before
                near = near + up_before * get(start_ref, k - 1)
            up_before = up
            if k == 0:
                total = total + weight * get(column_ref, 1)
                near = near + (1.0 - weight) * get(column_ref, 2)
            if k == 5:
                total = total + (1.0 - weight) * get(column_ref, 1)
                near = near + weight * get(column_ref, 2)
            inv = 1.0 / jnp.maximum(total, TINY)
            r = near - total * x
            z = r * inv
            put(inv_ref, k, i, inv)
            put(z0_ref, k, i, z)
            if sums is not None and k < 3:
                put_own(inv_out, k, i, inv)
                put_own(r0_out, k, i, r)
                energy = energy + fold(z * r)
        return None if sums is None else (energy,)

    def step(source, target, out, planes):
        def body(i, sums):
            def get(ref, k, off=0):
                return ref[k, :, pl.ds(OWN + 8 * i + off, 8), :]

            totals = sums
            up_before, z_before = None, None
            z = get(source, 0)
            for k in range(planes):
                col = get(col_link, k)
                near = get(row_link, k) * get(source, k, 1) + get(row_link, k, -1) * get(source, k, -1)
                near = near + col * after_col(z) + before_col(col * z)
                if k < 5:
                    up, z_after = get(up_link, k), get(source, k + 1)
                    near = near + up * z_after
                if k > 0:
                    near = near + up_before * z_before
                if target is not None:
                    fresh = near * get(inv_ref, k)
                    put(target, k, i, fresh)
                if sums is not None and k < 3:
                    put_own(out, k, i, near)
                    terms = (z * near,) if target is None else (z * near, fresh * near)
                    totals = tuple(a + fold(b) for a, b in zip(totals, terms))
                up_before, z_before, z = up, z, z_after
            return totals

        return body

    sums = sweep(first, 1)
    sums += sweep(step(z0_ref, z1_ref, s1_out, 5), 2)
    sums += sweep(step(z1_ref, z2_ref, s2_out, 4), 2)
    zero = jnp.zeros((8, LANES), jnp.float32)
    sums += lax.fori_loop(0, strips, step(z2_ref, None, s3_out, 3), (zero,))
    lane = lax.broadcasted_iota(jnp.int32, (8, LANES), 1)
    packed = zero
    for k, total in enumerate(sums):
        packed = jnp.where(lane == k, jnp.sum(total, keepdims=True), packed)
    moments_ref[...] = jnp.broadcast_to(packed[:1], moments_ref.shape)


def basis(devices, *operands):
    own = operands[1].shape
    shape = (own[2] // LANES + 1, own[1] + 2 * OWN, LANES)
    planes = (6, 6, 3, 6, 6, 5, 6, 6, 5, 4)
    return pl.pallas_call(
        basis_kernel,
        out_shape=(jax.ShapeDtypeStruct(own, jnp.float32),) * 5
        + (jax.ShapeDtypeStruct((devices, LANES), jnp.float32),),
        in_specs=[SMEM] + [VMEM] * (len(operands) - 1),
        out_specs=(VMEM,) * 6,
        scratch_shapes=[pltpu.VMEM((count,) + shape, jnp.float32) for count in planes],
        compiler_params=params(32),
        name="basis",
    )(*operands)


def product(one, two, moments):
    total = 0.0
    for i, a in enumerate(one):
        for j, b in enumerate(two):
            total = total + a * b * moments[i + j]
    return total


def coefficients(moments, iterations):
    drops = [moments[i] - moments[i + 1] for i in range(MOMENTS - 1)]
    one = jnp.ones_like(moments[0])
    residual, direction, iterate = [one], [one], [0.0 * one] * iterations
    energy = moments[0]
    for iteration in range(iterations):
        step = energy / product(direction, direction, drops)
        iterate = [x + step * (direction[i] if i < len(direction) else 0.0) for i, x in enumerate(iterate)]
        image = [a - b for a, b in zip(direction + [0.0], [0.0] + direction)]
        residual = [a - step * b for a, b in zip(residual + [0.0], image)]
        if iteration + 1 < iterations:
            after = product(residual, residual, moments)
            ratio = after / energy
            direction = [a + ratio * b for a, b in zip(residual, direction + [0.0])]
            energy = after
    return iterate, residual


def update_kernel(flag, sums, start, inv, r0_ref, s1_ref, s2_ref, s3_ref, drop_ref, residual_ref):
    sums = jnp.sum(sums[...], axis=0, keepdims=True)
    lane = lax.broadcasted_iota(jnp.int32, sums.shape, 1)
    moments = [
        jnp.sum(jnp.where(lane == k, sums, 0.0), axis=1, keepdims=True) for k in range(MOMENTS)
    ]
    x, r = coefficients(moments, 3)
    for k in range(3):
        index = jnp.where(flag[0] == 1, 2 - k, k)
        r0, s1, s2 = r0_ref[k], s1_ref[k], s2_ref[k]
        drop_ref[index] = start[index] + inv[k] * (x[0] * r0 + x[1] * s1 + x[2] * s2)
        residual_ref[index] = r[0] * r0 + r[1] * s1 + r[2] * s2 + r[3] * s3_ref[k]


def update(*operands):
    shape = jax.ShapeDtypeStruct(operands[2].shape, jnp.float32)
    return pl.pallas_call(
        update_kernel,
        out_shape=(shape, shape),
        in_specs=[SMEM] + [VMEM] * (len(operands) - 1),
        out_specs=(VMEM, VMEM),
        compiler_params=params(24),
        name="update",
    )(*operands)


def ring(value, axes, shift):
    count = lax.axis_size(axes)
    return lax.ppermute(value, axes, [(i, (i + shift) % count) for i in range(count)])


def per_device(profiles, time_weight, slot_cell, inst_count, metal, via_density, pad, start_drop):
    rows, cols = metal.shape[1], metal.shape[2]
    gx, gy, layer = lax.axis_index("gx"), lax.axis_index(GY), lax.axis_index("layer")
    flag = jnp.stack(
        [
            layer,
            gx > 0,
            gx < lax.axis_size("gx") - 1,
            gy > 0,
            gy < lax.axis_size(GY) - 1,
        ]
    ).astype(jnp.int32)
    other_metal = ring(metal, "layer", 1)
    other_start = ring(start_drop, "layer", 1)
    mine = scatter(profiles, time_weight, slot_cell, inst_count, (rows, cols))
    theirs = ring(mine, "layer", 1)
    planes = (flag, metal, other_metal, start_drop, other_start, via_density, pad, mine, theirs)
    first, last = strip_call(rows_kernel, (64, cols), "rows", *planes)
    after, before = ring(first, "gx", -1), ring(last, "gx", 1)
    first, last = strip_call(cols_kernel, (rows + 16, LANES), "cols", *planes, after, before)
    right, left = ring(first, GY, -1), ring(last, GY, 1)
    devices = lax.axis_size(ALL)
    inv, r0, s1, s2, s3, moments = basis(devices, *planes, after, before, right, left)
    sums = lax.all_to_all(moments, ALL, 0, 0, tiled=True)
    return update(flag, sums, start_drop, inv, r0, s1, s2, s3)


def solution(mesh):
    split = Mesh(
        mesh.devices.reshape(mesh.shape["gx"], 4, 8, mesh.shape["layer"]),
        ("gx", "gy_0", "gy_1", "layer"),
    )
    grid = P("layer", "gx", GY)
    return jax.shard_map(
        per_device,
        mesh=split,
        in_specs=(P("layer", "gx", GY, None), P(), grid, grid, grid, P("gx", GY), P("gx", GY), grid),
        out_specs=(grid, grid),
        check_vma=False,
    )
```

```python
import jax
import jax.numpy as jnp
from jax import lax
from jax.experimental import pallas as pl
from jax.experimental.pallas import tpu as pltpu
from jax.sharding import Mesh
from jax.sharding import PartitionSpec as P

ALL = ("gx", "gy_0", "gy_1", "layer")
GY = ("gy_0", "gy_1")
HALO = 4
LANES = 128
SIDE = 256
CHUNK = 4096
TINY = 1e-30
MOMENTS = 6

VMEM = pl.BlockSpec(memory_space=pltpu.VMEM)
HBM = pl.BlockSpec(memory_space=pltpu.HBM)
SMEM = pl.BlockSpec(memory_space=pltpu.SMEM)


def params(mebibytes):
    return pltpu.CompilerParams(vmem_limit_bytes=mebibytes << 20)


def scatter_kernel(count_ref, weight_ref, profile_hbm, cell_hbm, out_ref, profile_ref, cell_ref, total_ref, sems):
    half = out_ref.shape[0]
    blocks = profile_ref.shape[0] // CHUNK
    fetches = [pltpu.make_async_copy(cell_hbm, cell_ref, sems.at[blocks])]
    for block in range(blocks):
        span = pl.ds(block * CHUNK, CHUNK)
        fetches.append(
            pltpu.make_async_copy(profile_hbm.at[span], profile_ref.at[span], sems.at[block])
        )
    for fetch in fetches:
        fetch.start()
    total_ref[...] = jnp.zeros_like(total_ref)
    times = weight_ref.shape[0]
    weight = jnp.broadcast_to(weight_ref[...].reshape(1, times), (16, times))
    ids = lax.broadcasted_iota(jnp.int32, (SIDE, CHUNK), 0).astype(jnp.float32).astype(jnp.bfloat16)
    zero, one = jnp.bfloat16(0), jnp.bfloat16(1)
    fetches[0].wait()

    def add_block(block, _):
        first = pl.multiple_of(block * CHUNK, CHUNK)
        span = pl.ds(first, CHUNK)
        pltpu.make_async_copy(profile_hbm.at[span], profile_ref.at[span], sems.at[block]).wait()
        amount = lax.dot_general(
            weight,
            profile_ref[span, :],
            (((1,), (1,)), ((), ())),
            preferred_element_type=jnp.float32,
        )[:1]
        position = first + lax.broadcasted_iota(jnp.int32, (1, CHUNK), 1)
        amount = jnp.where(position < count_ref[0], amount, 0.0)
        high = amount.astype(jnp.bfloat16)
        low = (amount - high.astype(jnp.float32)).astype(jnp.bfloat16)
        cell = cell_ref[:, span]
        row = ((cell >> 9) + ((cell >> 8) & 1) * half).astype(jnp.float32).astype(jnp.bfloat16)
        col = (cell & (SIDE - 1)).astype(jnp.float32).astype(jnp.bfloat16)
        here = ids == row
        left = jnp.concatenate([jnp.where(here, high, zero), jnp.where(here, low, zero)], axis=0)
        right = jnp.where(ids == col, one, zero)
        total_ref[...] += lax.dot_general(
            left, right, (((1,), (1,)), ((), ())), preferred_element_type=jnp.float32
        )
        return 0

    lax.fori_loop(0, blocks, add_block, 0)
    both = total_ref[:SIDE, :] + total_ref[SIDE:, :]
    out_ref[:, :SIDE] = both[:half]
    out_ref[:, SIDE:] = both[half:]


def scatter(profiles, time_weight, slot_cell, inst_count, tile):
    slots, times = profiles.shape[-2:]
    return pl.pallas_call(
        scatter_kernel,
        out_shape=jax.ShapeDtypeStruct(tile, jnp.float32),
        in_specs=[SMEM, VMEM, HBM, HBM],
        out_specs=VMEM,
        scratch_shapes=[
            pltpu.VMEM((slots, times), jnp.bfloat16),
            pltpu.VMEM((1, slots), jnp.int32),
            pltpu.VMEM((2 * SIDE, SIDE), jnp.float32),
            pltpu.SemaphoreType.DMA((slots // CHUNK + 1,)),
        ],
        compiler_params=params(24),
        cost_estimate=pl.CostEstimate(
            flops=6 * slots * SIDE * SIDE, bytes_accessed=2 * slots * times, transcendentals=0
        ),
        name="scatter",
    )(
        inst_count.reshape(1),
        time_weight,
        pltpu.with_memory_space_constraint(profiles.reshape(slots, times), pltpu.HBM),
        pltpu.with_memory_space_constraint(slot_cell.reshape(1, slots), pltpu.HBM),
    )


def plane_readers(metal, other_metal, start, other_start, via, pad, mine, theirs, flip):
    readers = []
    for own, other in ((metal, other_metal), (start, other_start)):
        for ref in (own, other):
            for k in range(3):
                index = jnp.where(flip == 1, 2 - k, k)
                readers.append(lambda rows, cols, ref=ref, index=index: ref[index, rows, cols])
    readers.append(lambda rows, cols: via[rows, cols])
    readers.append(lambda rows, cols: pad[rows, cols])
    readers.append(lambda rows, cols: mine[rows, cols] + theirs[rows, cols])
    return readers


def rows_kernel(flag, m, om, s, os, via, pad, mine, theirs, one_ref, two_ref):
    rows = m.shape[1]
    readers = plane_readers(m, om, s, os, via, pad, mine, theirs, flag[0])
    low = lax.broadcasted_iota(jnp.int32, (8, m.shape[2]), 0) < HALO
    for pair in range(0, len(readers), 2):
        packed = []
        for start in (0, rows - 8):
            span = slice(start, start + 8)
            here = readers[pair](span, slice(None))
            there = here
            if pair + 1 < len(readers):
                there = pltpu.roll(readers[pair + 1](span, slice(None)), HALO, 0)
            packed.append(jnp.where(low, here, there) if start == 0 else jnp.where(low, there, here))
        first, last = packed
        span = slice(pair * HALO, pair * HALO + 8)
        one_ref[span, :] = jnp.where(flag[5] == 1, first, last)
        two_ref[span, :] = jnp.where(flag[5] == 1, last, first)


def row_halos(one, two, plane, cols, flag):
    span = slice(plane // 2 * 8, plane // 2 * 8 + 8)
    one, two = one[span, cols], two[span, cols]
    above = jnp.where(flag[1] == 1, jnp.where(flag[5] == 1, one, two), 0.0)
    below = jnp.where(flag[2] == 1, jnp.where(flag[5] == 1, two, one), 0.0)
    if plane % 2:
        return pltpu.roll(above, HALO, 0), pltpu.roll(below, HALO, 0)
    return above, below


def cols_kernel(flag, m, om, s, os, via, pad, mine, theirs, rows_one, rows_two, one_ref, two_ref):
    rows, cols = m.shape[1], m.shape[2]
    readers = plane_readers(m, om, s, os, via, pad, mine, theirs, flag[0])
    lane = lax.broadcasted_iota(jnp.int32, (rows + 16, LANES), 1)
    sides = []
    for start in (0, cols - LANES):
        span = slice(start, start + LANES)
        packed = jnp.zeros((rows + 16, LANES), jnp.float32)
        for plane, read in enumerate(readers):
            above, below = row_halos(rows_one, rows_two, plane, span, flag)
            values = jnp.concatenate([above, read(slice(None), span), below], axis=0)
            where = HALO * plane if start == 0 else (LANES - HALO + HALO * plane) % LANES
            turned = pltpu.roll(values, HALO * plane, 1) if plane else values
            packed = jnp.where((lane >= where) & (lane < where + HALO), turned, packed)
        sides.append(packed)
    first, last = sides
    one_ref[...] = jnp.where(flag[6] == 1, first, last)
    two_ref[...] = jnp.where(flag[6] == 1, last, first)


def col_halo(one, two, plane, flag):
    after = jnp.where(flag[6] == 1, two[...], one[...])
    before = jnp.where(flag[6] == 1, one[...], two[...])
    lane = lax.broadcasted_iota(jnp.int32, after.shape, 1)
    where = HALO * plane
    back = (LANES - HALO + where) % LANES
    tail = (lane >= where) & (lane < where + HALO) & (flag[4] == 1)
    head = (lane >= back) & (lane < back + HALO) & (flag[3] == 1)
    values = jnp.where(tail, after, jnp.where(head, before, 0.0))
    return pltpu.roll(values, (LANES - where) % LANES, 1) if plane else values


def strip_call(kernel, shape, name, *operands):
    return pl.pallas_call(
        kernel,
        out_shape=(jax.ShapeDtypeStruct(shape, jnp.float32),) * 2,
        in_specs=[SMEM] + [VMEM] * (len(operands) - 1),
        out_specs=(VMEM, VMEM),
        compiler_params=params(24),
        name=name,
    )(*operands)


OWN = 16


def harmonic(values, beside):
    return 2.0 * values * beside / jnp.maximum(values + beside, TINY)


def row_span(i, off=0):
    return pl.ds(OWN + 8 * i + off, 8)


def links_kernel(
    flag, m, om, s, os, via, pad, mine, theirs, rows_one, rows_two,
    row_link, col_link, up_link, total_ref, r_ref, metal_side, start_side,
    metal_ref, start_ref, column_ref,
):
    rows, cols = m.shape[1], m.shape[2]
    tiles, strips = cols // LANES, rows // 8
    readers = plane_readers(m, om, s, os, via, pad, mine, theirs, flag[0])
    places = [(metal_ref, k) for k in range(6)] + [(start_ref, k) for k in range(6)]
    places += [(column_ref, k) for k in range(3)]
    for plane, (read, (ref, k)) in enumerate(zip(readers, places)):
        for j in range(tiles):
            span = slice(j * LANES, j * LANES + LANES)
            above, below = row_halos(rows_one, rows_two, plane, span, flag)
            ref[k, j, OWN - 8 : OWN, :] = above
            ref[k, j, OWN : OWN + rows, :] = read(slice(None), span)
            ref[k, j, OWN + rows : OWN + rows + 8, :] = below

    lane = lax.broadcasted_iota(jnp.int32, (tiles, 8, LANES), 2)
    none = jnp.zeros((1, 8, LANES), jnp.float32)
    weight = jnp.where(flag[0] == 1, 1.0, 0.0)

    def after_col(values):
        turned = pltpu.roll(values, LANES - 1, 2)
        return jnp.where(lane == LANES - 1, jnp.concatenate([turned[1:], none], 0), turned)

    def before_col(values):
        turned = pltpu.roll(values, 1, 2)
        return jnp.where(lane == 0, jnp.concatenate([none, turned[:-1]], 0), turned)

    def body(i, _):
        i = i - 1

        def get(ref, k, off=0):
            return ref[k, :, row_span(i, off), :]

        up, metal, x = None, get(metal_ref, 0), get(start_ref, 0)
        x_before = None
        for k in range(6):
            row = harmonic(metal, get(metal_ref, k, 1))
            row_link[k, :, row_span(i), :] = row
            row_before = get(row_link, k, -1)
            col = harmonic(metal, after_col(metal))
            col_link[k, :, row_span(i), :] = col
            total = row + row_before + col + before_col(col)
            near = row * get(start_ref, k, 1) + row_before * get(start_ref, k, -1)
            near = near + col * after_col(x) + before_col(col * x)
            if k > 0:
                total = total + up
                near = near + up * x_before
            metal_side[k, :, row_span(i), :] = jnp.concatenate([metal[:1], metal[-1:]], 0)
            start_side[k, :, row_span(i), :] = jnp.concatenate([x[:1], x[-1:]], 0)
            x_here = x
            if k < 5:
                metal_after, x = get(metal_ref, k + 1), get(start_ref, k + 1)
                up = get(column_ref, 0) * harmonic(metal, metal_after)
                metal = metal_after
                up_link[k, :, row_span(i), :] = up
                total = total + up
                near = near + up * x
            if k == 0:
                total = total + weight * get(column_ref, 1)
                near = near + (1.0 - weight) * get(column_ref, 2)
            if k == 5:
                total = total + (1.0 - weight) * get(column_ref, 1)
                near = near + weight * get(column_ref, 2)
            total_ref[k, :, row_span(i), :] = total
            r_ref[k, :, row_span(i), :] = near - total * x_here
            x_before = x_here
        return 0

    lax.fori_loop(0, strips + 2, body, 0)


def links(*operands):
    own = operands[1].shape
    counts = [(6, 4), (6, 4), (5, 4), (6, 4), (6, 4), (6, 2), (6, 2)]
    height = own[1] + 2 * OWN
    return pl.pallas_call(
        links_kernel,
        out_shape=[jax.ShapeDtypeStruct(c + (height, LANES), jnp.float32) for c in counts],
        in_specs=[SMEM] + [VMEM] * (len(operands) - 1),
        out_specs=[VMEM] * len(counts),
        scratch_shapes=[pltpu.VMEM((count, 4, height, LANES), jnp.float32) for count in (6, 6, 3)],
        compiler_params=params(24),
        cost_estimate=pl.CostEstimate(flops=80_000_000, bytes_accessed=12_000_000, transcendentals=2_000_000),
        name="links",
    )(*operands)


def basis_kernel(
    flag, cols_one, cols_two, row_link, col_link, up_link, total_ref, r_ref, metal_side, start_side,
    inv_out, r0_out, s1_out, s2_out, s3_out, moments_ref,
    metal_ref, start_ref, column_ref, row_far, col_last, col_far, up_far, inv_ref, z0_ref, z1_ref, z2_ref,
):
    rows, tiles = inv_out.shape[1], col_link.shape[1]
    strips = rows // 8
    inner = slice(OWN - 8, OWN + rows + 8)
    for plane in range(15):
        ref = (metal_ref, start_ref, column_ref)[plane // 6]
        ref[plane % 6, inner, :] = col_halo(cols_one, cols_two, plane, flag)

    weight = jnp.where(flag[0] == 1, 1.0, 0.0)
    lane = lax.broadcasted_iota(jnp.int32, (8, LANES), 1)
    zero = jnp.zeros((8, LANES), jnp.float32)

    def later(values):
        return pltpu.roll(values, LANES - 1, values.ndim - 1)

    def earlier(values):
        return pltpu.roll(values, 1, values.ndim - 1)

    def put_own(ref, k, i, values):
        for j in range(tiles):
            ref[k, pl.ds(8 * i, 8), j * LANES : j * LANES + LANES] = values[j]

    def fold(values):
        return jnp.sum(values[:tiles], axis=0)

    def sweep(body, count):
        body(-1, None)
        sums = lax.fori_loop(0, strips, body, (zero,) * count)
        body(strips, None)
        return sums

    def first(i, sums):
        def get(ref, k, off=0):
            return ref[k, row_span(i, off), :]

        energy = None if sums is None else sums[0]
        up = None
        for k in range(6):
            metal, x = get(metal_ref, k), get(start_ref, k)
            metal_first, metal_last = metal_side[k, 0, row_span(i), :], metal_side[k, 1, row_span(i), :]
            x_first, x_last = start_side[k, 0, row_span(i), :], start_side[k, 1, row_span(i), :]
            row = harmonic(metal, get(metal_ref, k, 1))
            row_far[k, row_span(i), :] = row
            row_before = get(row_far, k, -1)
            metal_later = later(metal)
            last = jnp.where(lane == LANES - 1, harmonic(metal_last, metal_later), 0.0)
            col_last[k, row_span(i), :] = col_link[k, tiles - 1, row_span(i), :] + last
            col = harmonic(metal, jnp.where(lane == LANES - 1, later(metal_first), metal_later))
            col_far[k, row_span(i), :] = col
            col_earlier, x_later = earlier(col), later(x)
            total = row + row_before + col + jnp.where(lane == 0, earlier(last), col_earlier)
            near = row * get(start_ref, k, 1) + row_before * get(start_ref, k, -1)
            near = near + col * jnp.where(lane == LANES - 1, later(x_first), x_later)
            near = near + jnp.where(lane == 0, earlier(last * x_last), earlier(col * x))
            if k > 0:
                total = total + up
                near = near + up * get(start_ref, k - 1)
            if k < 5:
                up = get(column_ref, 0) * harmonic(metal, get(metal_ref, k + 1))
                up_far[k, row_span(i), :] = up
                total = total + up
                near = near + up * get(start_ref, k + 1)
            if k == 0:
                total = total + weight * get(column_ref, 1)
                near = near + (1.0 - weight) * get(column_ref, 2)
            if k == 5:
                total = total + (1.0 - weight) * get(column_ref, 1)
                near = near + weight * get(column_ref, 2)
            before = jnp.where(lane == 0, col_earlier, 0.0)
            totals, r = total_ref[k, :, row_span(i), :], r_ref[k, :, row_span(i), :]
            totals = [totals[0] + before, totals[1], totals[2], totals[3] + last, total]
            r = [
                r[0] + before * (earlier(x) - x_first),
                r[1],
                r[2],
                r[3] + last * (x_later - x_last),
                near - total * x,
            ]
            inv, r = 1.0 / jnp.maximum(jnp.stack(totals), TINY), jnp.stack(r)
            z = r * inv
            inv_ref[k, :, row_span(i), :] = inv
            z0_ref[k, :, row_span(i), :] = z
            if sums is not None and k < 3:
                put_own(inv_out, k, i, inv)
                put_own(r0_out, k, i, r)
                energy = energy + fold(z * r)
        return None if sums is None else (energy,)

    def step(source, target, out, planes):
        width = tiles if target is None else tiles + 1
        ends = lax.broadcasted_iota(jnp.int32, (width, 8, LANES), 2)

        def body(i, sums):
            def get(k, off=0):
                return source[k, :width, row_span(i, off), :]

            def whole(near_ref, far_ref, k, off=0):
                near = near_ref[k, :, row_span(i, off), :]
                if width == tiles:
                    return near
                return jnp.concatenate([near, far_ref[k, row_span(i, off), :][None]], 0)

            totals = sums
            up, z_before = None, None
            z = source[0, :, row_span(i), :]
            for k in range(planes):
                col = jnp.concatenate(
                    [
                        col_link[k, : tiles - 1, row_span(i), :],
                        col_last[k, row_span(i), :][None],
                        col_far[k, row_span(i), :][None],
                    ],
                    0,
                )
                turned = later(z)
                following = jnp.concatenate([turned[1:], turned[:1]], 0)
                z_later = jnp.where(ends == LANES - 1, following[:width], turned[:width])
                turned = earlier(col * z)
                preceding = jnp.concatenate([turned[-1:], turned[:-1]], 0)
                near = col[:width] * z_later + jnp.where(ends == 0, preceding[:width], turned[:width])
                near = near + whole(row_link, row_far, k) * get(k, 1)
                near = near + whole(row_link, row_far, k, -1) * get(k, -1)
                if k > 0:
                    near = near + up * z_before
                z_after = source[k + 1, :, row_span(i), :]
                up = whole(up_link, up_far, k) if k < 5 else None
                if k < 5:
                    near = near + up * z_after[:width]
                z_here = z[:width]
                if target is not None:
                    fresh = near * inv_ref[k, :, row_span(i), :]
                    target[k, :, row_span(i), :] = fresh
                if sums is not None and k < 3:
                    put_own(out, k, i, near)
                    terms = (z_here * near,) if target is None else (z_here * near, fresh * near)
                    totals = tuple(a + fold(b) for a, b in zip(totals, terms))
                z_before, z = z_here, z_after
            return totals

        return body

    sums = sweep(first, 1)
    sums += sweep(step(z0_ref, z1_ref, s1_out, 5), 2)
    sums += sweep(step(z1_ref, z2_ref, s2_out, 4), 2)
    sums += lax.fori_loop(0, strips, step(z2_ref, None, s3_out, 3), (zero,))
    packed = zero
    for k, total in enumerate(sums):
        packed = jnp.where(lane == k, jnp.sum(total, keepdims=True), packed)
    moments_ref[...] = jnp.broadcast_to(packed[:1], moments_ref.shape)


def basis(devices, own, *operands):
    height = own[1] + 2 * OWN
    sides = (6, 6, 3, 6, 6, 6, 5)
    planes = (6, 6, 5, 4)
    return pl.pallas_call(
        basis_kernel,
        out_shape=(jax.ShapeDtypeStruct(own, jnp.float32),) * 5
        + (jax.ShapeDtypeStruct((devices, LANES), jnp.float32),),
        in_specs=[SMEM] + [VMEM] * (len(operands) - 1),
        out_specs=(VMEM,) * 6,
        scratch_shapes=[pltpu.VMEM((count, height, LANES), jnp.float32) for count in sides]
        + [pltpu.VMEM((count, 5, height, LANES), jnp.float32) for count in planes],
        compiler_params=params(20),
        name="basis",
    )(*operands)


def product(one, two, moments):
    total = 0.0
    for i, a in enumerate(one):
        for j, b in enumerate(two):
            total = total + a * b * moments[i + j]
    return total


def coefficients(moments, iterations):
    drops = [moments[i] - moments[i + 1] for i in range(MOMENTS - 1)]
    one = jnp.ones_like(moments[0])
    residual, direction, iterate = [one], [one], [0.0 * one] * iterations
    energy = moments[0]
    for iteration in range(iterations):
        step = energy / product(direction, direction, drops)
        iterate = [x + step * (direction[i] if i < len(direction) else 0.0) for i, x in enumerate(iterate)]
        image = [a - b for a, b in zip(direction + [0.0], [0.0] + direction)]
        residual = [a - step * b for a, b in zip(residual + [0.0], image)]
        if iteration + 1 < iterations:
            after = product(residual, residual, moments)
            ratio = after / energy
            direction = [a + ratio * b for a, b in zip(residual, direction + [0.0])]
            energy = after
    return iterate, residual


def update_kernel(
    flag, sums, start, inv, r0_ref, s1_ref, s2_ref, s3_ref, drop_out, residual_out, drop_ref, residual_ref, sems
):
    sums = jnp.sum(sums[...], axis=0, keepdims=True)
    lane = lax.broadcasted_iota(jnp.int32, sums.shape, 1)
    moments = [
        jnp.sum(jnp.where(lane == k, sums, 0.0), axis=1, keepdims=True) for k in range(MOMENTS)
    ]
    x, r = coefficients(moments, 3)
    copies = []
    for k in range(3):
        index = jnp.where(flag[0] == 1, 2 - k, k)
        r0, s1, s2 = r0_ref[k], s1_ref[k], s2_ref[k]
        drop_ref[k] = start[index] + inv[k] * (x[0] * r0 + x[1] * s1 + x[2] * s2)
        residual_ref[k] = r[0] * r0 + r[1] * s1 + r[2] * s2 + r[3] * s3_ref[k]
        copies.append(pltpu.make_async_copy(drop_ref.at[k], drop_out.at[index], sems.at[2 * k]))
        copies.append(pltpu.make_async_copy(residual_ref.at[k], residual_out.at[index], sems.at[2 * k + 1]))
        for copy in copies[-2:]:
            copy.start()
    for copy in copies:
        copy.wait()


def update(*operands):
    own = operands[2].shape
    shape = jax.ShapeDtypeStruct(own, jnp.float32)
    return pl.pallas_call(
        update_kernel,
        out_shape=(shape, shape),
        in_specs=[SMEM] + [VMEM] * (len(operands) - 1),
        out_specs=(HBM, HBM),
        scratch_shapes=[
            pltpu.VMEM(own, jnp.float32),
            pltpu.VMEM(own, jnp.float32),
            pltpu.SemaphoreType.DMA((6,)),
        ],
        compiler_params=params(24),
        name="update",
    )(*operands)


def trade(one, two, axes):
    count = lax.axis_size(axes)
    pairs = [(i, i ^ 1) for i in range(count)]
    shifted = [((i + 1) % count, (j + 1) % count) for i, j in pairs]
    return lax.ppermute(one, axes, pairs), lax.ppermute(two, axes, shifted)


def swap(value):
    return lax.ppermute(value, "layer", [(0, 1), (1, 0)])


def per_device(profiles, time_weight, slot_cell, inst_count, metal, via_density, pad, start_drop):
    rows, cols = metal.shape[1], metal.shape[2]
    gx, gy, layer = lax.axis_index("gx"), lax.axis_index(GY), lax.axis_index("layer")
    flag = jnp.stack(
        [
            layer,
            gx > 0,
            gx < lax.axis_size("gx") - 1,
            gy > 0,
            gy < lax.axis_size(GY) - 1,
            gx % 2,
            gy % 2,
        ]
    ).astype(jnp.int32)
    other_metal = swap(metal)
    other_start = swap(start_drop)
    mine = scatter(profiles, time_weight, slot_cell, inst_count, (rows, cols))
    theirs = swap(mine)
    planes = (flag, metal, other_metal, start_drop, other_start, via_density, pad, mine, theirs)
    row_strips = trade(*strip_call(rows_kernel, (64, cols), "rows", *planes), "gx")
    col_strips = trade(*strip_call(cols_kernel, (rows + 16, LANES), "cols", *planes, *row_strips), GY)
    prepared = links(*planes, *row_strips)
    devices = lax.axis_size(ALL)
    inv, r0, s1, s2, s3, moments = basis(devices, metal.shape, flag, *col_strips, *prepared)
    sums = lax.all_to_all(moments, ALL, 0, 0, tiled=True)
    return update(flag, sums, start_drop, inv, r0, s1, s2, s3)


def solution(mesh):
    split = Mesh(
        mesh.devices.reshape(mesh.shape["gx"], 4, 8, mesh.shape["layer"]),
        ("gx", "gy_0", "gy_1", "layer"),
    )
    grid = P("layer", "gx", GY)
    return jax.shard_map(
        per_device,
        mesh=split,
        in_specs=(P("layer", "gx", GY, None), P(), grid, grid, grid, P("gx", GY), P("gx", GY), grid),
        out_specs=(grid, grid),
        check_vma=False,
    )
```

```python
import jax
import jax.numpy as jnp
from jax import lax
from jax.experimental import pallas as pl
from jax.experimental.pallas import tpu as pltpu
from jax.sharding import Mesh
from jax.sharding import PartitionSpec as P

ALL = ("gx", "gy_0", "gy_1", "layer")
GY = ("gy_0", "gy_1")
HALO = 4
LANES = 128
SIDE = 256
CHUNK = 4096
TINY = 1e-30
MOMENTS = 6

VMEM = pl.BlockSpec(memory_space=pltpu.VMEM)
HBM = pl.BlockSpec(memory_space=pltpu.HBM)
SMEM = pl.BlockSpec(memory_space=pltpu.SMEM)


def params(mebibytes):
    return pltpu.CompilerParams(vmem_limit_bytes=mebibytes << 20)


def scatter_kernel(
    count_ref, weight_hbm, profile_hbm, cell_hbm,
    out_ref, weight_ref, profile_ref, cell_ref, total_ref, sems,
):
    half = out_ref.shape[0]
    blocks = profile_ref.shape[0] // CHUNK
    fetches = [
        pltpu.make_async_copy(cell_hbm, cell_ref, sems.at[blocks]),
        pltpu.make_async_copy(weight_hbm, weight_ref, sems.at[blocks + 1]),
    ]
    for block in range(blocks):
        span = pl.ds(block * CHUNK, CHUNK)
        fetches.append(
            pltpu.make_async_copy(profile_hbm.at[span], profile_ref.at[span], sems.at[block])
        )
    for fetch in fetches:
        fetch.start()
    total_ref[...] = jnp.zeros_like(total_ref)
    ids = lax.broadcasted_iota(jnp.int32, (SIDE, CHUNK), 0).astype(jnp.float32).astype(jnp.bfloat16)
    zero, one = jnp.bfloat16(0), jnp.bfloat16(1)
    fetches[0].wait()
    fetches[1].wait()
    times = weight_ref.shape[0]
    weight = jnp.broadcast_to(weight_ref[...].reshape(1, times), (16, times))

    def add_block(block, _):
        first = pl.multiple_of(block * CHUNK, CHUNK)
        span = pl.ds(first, CHUNK)
        pltpu.make_async_copy(profile_hbm.at[span], profile_ref.at[span], sems.at[block]).wait()
        amount = lax.dot_general(
            weight,
            profile_ref[span, :],
            (((1,), (1,)), ((), ())),
            preferred_element_type=jnp.float32,
        )[:1]
        position = first + lax.broadcasted_iota(jnp.int32, (1, CHUNK), 1)
        amount = jnp.where(position < count_ref[0, 0, 0], amount, 0.0)
        high = amount.astype(jnp.bfloat16)
        low = (amount - high.astype(jnp.float32)).astype(jnp.bfloat16)
        cell = cell_ref[:, span]
        row = ((cell >> 9) + ((cell >> 8) & 1) * half).astype(jnp.float32).astype(jnp.bfloat16)
        col = (cell & (SIDE - 1)).astype(jnp.float32).astype(jnp.bfloat16)
        here = ids == row
        left = jnp.concatenate([jnp.where(here, high, zero), jnp.where(here, low, zero)], axis=0)
        right = jnp.where(ids == col, one, zero)
        total_ref[...] += lax.dot_general(
            left, right, (((1,), (1,)), ((), ())), preferred_element_type=jnp.float32
        )
        return 0

    lax.fori_loop(0, blocks, add_block, 0)
    both = total_ref[:SIDE, :] + total_ref[SIDE:, :]
    out_ref[:, :SIDE] = both[:half]
    out_ref[:, SIDE:] = both[half:]


def in_hbm(value):
    return pltpu.with_memory_space_constraint(value, pltpu.HBM)


def scatter(profiles, time_weight, slot_cell, inst_count, tile):
    slots, times = profiles.shape[-2:]
    return pl.pallas_call(
        scatter_kernel,
        out_shape=jax.ShapeDtypeStruct(tile, jnp.float32),
        in_specs=[SMEM, HBM, HBM, HBM],
        out_specs=VMEM,
        scratch_shapes=[
            pltpu.VMEM((times,), jnp.bfloat16),
            pltpu.VMEM((slots, times), jnp.bfloat16),
            pltpu.VMEM((1, slots), jnp.int32),
            pltpu.VMEM((2 * SIDE, SIDE), jnp.float32),
            pltpu.SemaphoreType.DMA((slots // CHUNK + 2,)),
        ],
        compiler_params=params(20),
        cost_estimate=pl.CostEstimate(
            flops=6 * slots * SIDE * SIDE, bytes_accessed=2 * slots * times, transcendentals=0
        ),
        name="scatter",
    )(
        inst_count,
        in_hbm(time_weight),
        in_hbm(profiles.reshape(slots, times)),
        in_hbm(slot_cell.reshape(1, slots)),
    )


PLANES = 15


class Reader:
    def __init__(self, read, shape):
        self.read, self.shape = read, shape

    def __call__(self, rows, cols):
        return self.read(rows, cols)


def plane_readers(metal, other_metal, start, other_start, via, pad, mine, theirs, flip):
    reads = []
    for own, other in ((metal, other_metal), (start, other_start)):
        for ref in (own, other):
            for k in range(3):
                index = jnp.where(flip == 1, 2 - k, k)
                reads.append(lambda rows, cols, ref=ref, index=index: ref[index, rows, cols])
    if via is not None:
        reads.append(lambda rows, cols: via[rows, cols])
        reads.append(lambda rows, cols: pad[rows, cols])
        reads.append(lambda rows, cols: mine[rows, cols] + theirs[rows, cols])
    return [Reader(read, metal.shape[1:]) for read in reads]


def row_strips(readers, first_plane, flag, one_ref, two_ref):
    rows, cols = readers[0].shape
    low = lax.broadcasted_iota(jnp.int32, (8, cols), 0) < HALO
    for pair in range(0, len(readers), 2):
        packed = []
        for start in (0, rows - 8):
            span = slice(start, start + 8)
            here = readers[pair](span, slice(None))
            there = here
            if pair + 1 < len(readers):
                there = pltpu.roll(readers[pair + 1](span, slice(None)), HALO, 0)
            packed.append(jnp.where(low, here, there) if start == 0 else jnp.where(low, there, here))
        first, last = packed
        start = (first_plane + pair) * HALO
        one_ref[start : start + 8, :] = jnp.where(flag[5] == 1, first, last)
        two_ref[start : start + 8, :] = jnp.where(flag[5] == 1, last, first)


def rows_kernel(flag, via_hbm, pad_hbm, m, om, s, os, one_ref, two_ref, edge_ref, sems):
    rows = m.shape[1]
    fetches = []
    for plane, ref in enumerate((via_hbm, pad_hbm)):
        for side, start in enumerate((0, rows - 8)):
            place = edge_ref.at[plane, pl.ds(8 * side, 8)]
            copy = pltpu.make_async_copy(ref.at[pl.ds(start, 8)], place, sems.at[2 * plane + side])
            copy.start()
            fetches.append(copy)

    def edge(plane):
        return lambda rows, cols: edge_ref[plane, (slice(0, 8) if rows.start == 0 else slice(8, 16)), cols]

    readers = plane_readers(m, om, s, os, None, None, None, None, flag[0])
    row_strips(readers, 0, flag, one_ref, two_ref)
    for fetch in fetches:
        fetch.wait()
    readers = [Reader(edge(plane), m.shape[1:]) for plane in range(2)]
    row_strips(readers, PLANES - 3, flag, one_ref, two_ref)


def fed_kernel(flag, mine, theirs, one_in, two_in, one_ref, two_ref):
    reader = Reader(lambda rows, cols: mine[rows, cols] + theirs[rows, cols], mine.shape)
    row_strips([reader], PLANES - 1, flag, one_ref, two_ref)


def row_halos(one, two, plane, cols, flag):
    span = slice(plane // 2 * 8, plane // 2 * 8 + 8)
    one, two = one[span, cols], two[span, cols]
    above = jnp.where(flag[1] == 1, jnp.where(flag[5] == 1, one, two), 0.0)
    below = jnp.where(flag[2] == 1, jnp.where(flag[5] == 1, two, one), 0.0)
    if plane % 2:
        return pltpu.roll(above, HALO, 0), pltpu.roll(below, HALO, 0)
    return above, below


def col_strips(values_of, height, cols, flag):
    lane = lax.broadcasted_iota(jnp.int32, (height, LANES), 1)
    sides = []
    for start in (0, cols - LANES):
        span = slice(start, start + LANES)
        packed = jnp.zeros((height, LANES), jnp.float32)
        for plane in range(PLANES):
            values = values_of(plane, span)
            where = HALO * plane if start == 0 else (LANES - HALO + HALO * plane) % LANES
            turned = pltpu.roll(values, HALO * plane, 1) if plane else values
            packed = jnp.where((lane >= where) & (lane < where + HALO), turned, packed)
        sides.append(packed)
    first, last = sides
    return jnp.where(flag[6] == 1, first, last), jnp.where(flag[6] == 1, last, first)


def cols_kernel(flag, m, om, s, os, via, pad, mine, theirs, one_ref, two_ref):
    rows, cols = via.shape
    readers = plane_readers(m, om, s, os, via, pad, mine, theirs, flag[0])
    inner = slice(8, 8 + rows)
    one_ref[inner, :], two_ref[inner, :] = col_strips(
        lambda plane, span: readers[plane](slice(None), span), rows, cols, flag
    )


def corners_kernel(flag, rows_one, rows_two, one_in, two_in, one_ref, two_ref):
    height, cols = one_ref.shape[0], rows_one.shape[1]

    def halos(plane, span):
        return jnp.concatenate(row_halos(rows_one, rows_two, plane, span, flag), axis=0)

    one, two = col_strips(halos, 16, cols, flag)
    for ref, values in ((one_ref, one), (two_ref, two)):
        ref[:8, :] = values[:8]
        ref[height - 8 :, :] = values[8:]


def col_halo_of(one, two, plane, flag):
    after = jnp.where(flag[6] == 1, two[...], one[...])
    before = jnp.where(flag[6] == 1, one[...], two[...])
    lane = lax.broadcasted_iota(jnp.int32, after.shape, 1)
    where = HALO * plane
    back = (LANES - HALO + where) % LANES
    tail = (lane >= where) & (lane < where + HALO) & (flag[4] == 1)
    head = (lane >= back) & (lane < back + HALO) & (flag[3] == 1)
    values = jnp.where(tail, after, jnp.where(head, before, 0.0))
    return pltpu.roll(values, (LANES - where) % LANES, 1) if plane else values


def strip_call(kernel, shape, name, *operands, in_place=False, far=0, scratch=()):
    last = len(operands) - 1
    return pl.pallas_call(
        kernel,
        out_shape=(jax.ShapeDtypeStruct(shape, jnp.float32),) * 2,
        in_specs=[SMEM] + [HBM] * far + [VMEM] * (last - far),
        out_specs=(VMEM, VMEM),
        scratch_shapes=scratch,
        input_output_aliases={last - 1: 0, last: 1} if in_place else {},
        compiler_params=params(8),
        cost_estimate=pl.CostEstimate(flops=2_000_000, bytes_accessed=1_000_000, transcendentals=0),
        name=name,
    )(*operands)


OWN = 16


def harmonic(values, beside):
    return 2.0 * values * beside / jnp.maximum(values + beside, TINY)


def row_span(i, off=0):
    return pl.ds(OWN + 8 * i + off, 8)


def links_kernel(
    flag, m, om, s, os, via, pad, mine, theirs, rows_one, rows_two,
    row_link, col_link, up_link, total_ref, r_ref, metal_side, start_side,
    metal_ref, start_ref, column_ref,
):
    rows, cols = m.shape[1], m.shape[2]
    tiles, strips = cols // LANES, rows // 8
    readers = plane_readers(m, om, s, os, via, pad, mine, theirs, flag[0])
    places = [(metal_ref, k) for k in range(6)] + [(start_ref, k) for k in range(6)]
    places += [(column_ref, k) for k in range(3)]
    for plane, (read, (ref, k)) in enumerate(zip(readers, places)):
        for j in range(tiles):
            span = slice(j * LANES, j * LANES + LANES)
            above, below = row_halos(rows_one, rows_two, plane, span, flag)
            ref[k, j, OWN - 8 : OWN, :] = above
            ref[k, j, OWN : OWN + rows, :] = read(slice(None), span)
            ref[k, j, OWN + rows : OWN + rows + 8, :] = below

    lane = lax.broadcasted_iota(jnp.int32, (tiles, 8, LANES), 2)
    none = jnp.zeros((1, 8, LANES), jnp.float32)
    weight = jnp.where(flag[0] == 1, 1.0, 0.0)

    def after_col(values):
        turned = pltpu.roll(values, LANES - 1, 2)
        return jnp.where(lane == LANES - 1, jnp.concatenate([turned[1:], none], 0), turned)

    def before_col(values):
        turned = pltpu.roll(values, 1, 2)
        return jnp.where(lane == 0, jnp.concatenate([none, turned[:-1]], 0), turned)

    def body(i, _):
        i = i - 1

        def get(ref, k, off=0):
            return ref[k, :, row_span(i, off), :]

        up, metal, x = None, get(metal_ref, 0), get(start_ref, 0)
        x_before = None
        for k in range(6):
            row = harmonic(metal, get(metal_ref, k, 1))
            row_link[k, :, row_span(i), :] = row
            row_before = get(row_link, k, -1)
            col = harmonic(metal, after_col(metal))
            col_link[k, :, row_span(i), :] = col
            total = row + row_before + col + before_col(col)
            near = row * get(start_ref, k, 1) + row_before * get(start_ref, k, -1)
            near = near + col * after_col(x) + before_col(col * x)
            if k > 0:
                total = total + up
                near = near + up * x_before
            metal_side[k, :, row_span(i), :] = jnp.concatenate([metal[:1], metal[-1:]], 0)
            start_side[k, :, row_span(i), :] = jnp.concatenate([x[:1], x[-1:]], 0)
            x_here = x
            if k < 5:
                metal_after, x = get(metal_ref, k + 1), get(start_ref, k + 1)
                up = get(column_ref, 0) * harmonic(metal, metal_after)
                metal = metal_after
                up_link[k, :, row_span(i), :] = up
                total = total + up
                near = near + up * x
            if k == 0:
                total = total + weight * get(column_ref, 1)
                near = near + (1.0 - weight) * get(column_ref, 2)
            if k == 5:
                total = total + (1.0 - weight) * get(column_ref, 1)
                near = near + weight * get(column_ref, 2)
            total_ref[k, :, row_span(i), :] = total
            r_ref[k, :, row_span(i), :] = near - total * x_here
            x_before = x_here
        return 0

    lax.fori_loop(0, strips + 2, body, 0)


def links(*operands):
    own = operands[1].shape
    counts = [(6, 4), (6, 4), (5, 4), (6, 4), (6, 4), (6, 2), (6, 2)]
    height = own[1] + 2 * OWN
    return pl.pallas_call(
        links_kernel,
        out_shape=[jax.ShapeDtypeStruct(c + (height, LANES), jnp.float32) for c in counts],
        in_specs=[SMEM] + [VMEM] * (len(operands) - 1),
        out_specs=[VMEM] * len(counts),
        scratch_shapes=[pltpu.VMEM((count, 4, height, LANES), jnp.float32) for count in (6, 6, 3)],
        compiler_params=params(24),
        cost_estimate=pl.CostEstimate(flops=80_000_000, bytes_accessed=12_000_000, transcendentals=2_000_000),
        name="links",
    )(*operands)


def basis_kernel(
    flag, cols_one, cols_two, row_link, col_link, up_link, total_ref, r_ref, metal_side, start_side,
    inv_out, r0_out, s1_out, s2_out, s3_out, moments_ref,
    metal_ref, start_ref, column_ref, row_far, col_last, col_far, up_far, inv_ref, z0_ref, z1_ref, z2_ref,
):
    rows, tiles = inv_out.shape[1], col_link.shape[1]
    strips = rows // 8
    inner = slice(OWN - 8, OWN + rows + 8)
    for plane in range(15):
        ref = (metal_ref, start_ref, column_ref)[plane // 6]
        ref[plane % 6, inner, :] = col_halo_of(cols_one, cols_two, plane, flag)

    weight = jnp.where(flag[0] == 1, 1.0, 0.0)
    lane = lax.broadcasted_iota(jnp.int32, (8, LANES), 1)
    zero = jnp.zeros((8, LANES), jnp.float32)

    def later(values):
        return pltpu.roll(values, LANES - 1, values.ndim - 1)

    def earlier(values):
        return pltpu.roll(values, 1, values.ndim - 1)

    def put_own(ref, k, i, values):
        for j in range(tiles):
            ref[k, pl.ds(8 * i, 8), j * LANES : j * LANES + LANES] = values[j]

    def fold(values):
        return jnp.sum(values[:tiles], axis=0)

    def sweep(body, count):
        body(-1, None)
        sums = lax.fori_loop(0, strips, body, (zero,) * count)
        body(strips, None)
        return sums

    def first(i, sums):
        def get(ref, k, off=0):
            return ref[k, row_span(i, off), :]

        energy = None if sums is None else sums[0]
        up = None
        for k in range(6):
            metal, x = get(metal_ref, k), get(start_ref, k)
            metal_first, metal_last = metal_side[k, 0, row_span(i), :], metal_side[k, 1, row_span(i), :]
            x_first, x_last = start_side[k, 0, row_span(i), :], start_side[k, 1, row_span(i), :]
            row = harmonic(metal, get(metal_ref, k, 1))
            row_far[k, row_span(i), :] = row
            row_before = get(row_far, k, -1)
            metal_later = later(metal)
            last = jnp.where(lane == LANES - 1, harmonic(metal_last, metal_later), 0.0)
            col_last[k, row_span(i), :] = col_link[k, tiles - 1, row_span(i), :] + last
            col = harmonic(metal, jnp.where(lane == LANES - 1, later(metal_first), metal_later))
            col_far[k, row_span(i), :] = col
            col_earlier, x_later = earlier(col), later(x)
            total = row + row_before + col + jnp.where(lane == 0, earlier(last), col_earlier)
            near = row * get(start_ref, k, 1) + row_before * get(start_ref, k, -1)
            near = near + col * jnp.where(lane == LANES - 1, later(x_first), x_later)
            near = near + jnp.where(lane == 0, earlier(last * x_last), earlier(col * x))
            if k > 0:
                total = total + up
                near = near + up * get(start_ref, k - 1)
            if k < 5:
                up = get(column_ref, 0) * harmonic(metal, get(metal_ref, k + 1))
                up_far[k, row_span(i), :] = up
                total = total + up
                near = near + up * get(start_ref, k + 1)
            if k == 0:
                total = total + weight * get(column_ref, 1)
                near = near + (1.0 - weight) * get(column_ref, 2)
            if k == 5:
                total = total + (1.0 - weight) * get(column_ref, 1)
                near = near + weight * get(column_ref, 2)
            before = jnp.where(lane == 0, col_earlier, 0.0)
            totals, r = total_ref[k, :, row_span(i), :], r_ref[k, :, row_span(i), :]
            totals = [totals[0] + before, totals[1], totals[2], totals[3] + last, total]
            r = [
                r[0] + before * (earlier(x) - x_first),
                r[1],
                r[2],
                r[3] + last * (x_later - x_last),
                near - total * x,
            ]
            inv, r = 1.0 / jnp.maximum(jnp.stack(totals), TINY), jnp.stack(r)
            z = r * inv
            inv_ref[k, :, row_span(i), :] = inv
            z0_ref[k, :, row_span(i), :] = z
            if sums is not None and k < 3:
                put_own(inv_out, k, i, inv)
                put_own(r0_out, k, i, r)
                energy = energy + fold(z * r)
        return None if sums is None else (energy,)

    def step(source, target, out, planes):
        width = tiles if target is None else tiles + 1
        ends = lax.broadcasted_iota(jnp.int32, (width, 8, LANES), 2)

        def body(i, sums):
            def get(k, off=0):
                return source[k, :width, row_span(i, off), :]

            def whole(near_ref, far_ref, k, off=0):
                near = near_ref[k, :, row_span(i, off), :]
                if width == tiles:
                    return near
                return jnp.concatenate([near, far_ref[k, row_span(i, off), :][None]], 0)

            totals = sums
            up, z_before = None, None
            z = source[0, :, row_span(i), :]
            for k in range(planes):
                col = jnp.concatenate(
                    [
                        col_link[k, : tiles - 1, row_span(i), :],
                        col_last[k, row_span(i), :][None],
                        col_far[k, row_span(i), :][None],
                    ],
                    0,
                )
                turned = later(z)
                following = jnp.concatenate([turned[1:], turned[:1]], 0)
                z_later = jnp.where(ends == LANES - 1, following[:width], turned[:width])
                turned = earlier(col * z)
                preceding = jnp.concatenate([turned[-1:], turned[:-1]], 0)
                near = col[:width] * z_later + jnp.where(ends == 0, preceding[:width], turned[:width])
                near = near + whole(row_link, row_far, k) * get(k, 1)
                near = near + whole(row_link, row_far, k, -1) * get(k, -1)
                if k > 0:
                    near = near + up * z_before
                z_after = source[k + 1, :, row_span(i), :]
                up = whole(up_link, up_far, k) if k < 5 else None
                if k < 5:
                    near = near + up * z_after[:width]
                z_here = z[:width]
                if target is not None:
                    fresh = near * inv_ref[k, :, row_span(i), :]
                    target[k, :, row_span(i), :] = fresh
                if sums is not None and k < 3:
                    put_own(out, k, i, near)
                    terms = (z_here * near,) if target is None else (z_here * near, fresh * near)
                    totals = tuple(a + fold(b) for a, b in zip(totals, terms))
                z_before, z = z_here, z_after
            return totals

        return body

    sums = sweep(first, 1)
    sums += sweep(step(z0_ref, z1_ref, s1_out, 5), 2)
    sums += sweep(step(z1_ref, z2_ref, s2_out, 4), 2)
    sums += lax.fori_loop(0, strips, step(z2_ref, None, s3_out, 3), (zero,))
    packed = zero
    for k, total in enumerate(sums):
        packed = jnp.where(lane == k, jnp.sum(total, keepdims=True), packed)
    moments_ref[...] = jnp.broadcast_to(packed[:1], moments_ref.shape)


def basis(devices, own, *operands):
    height = own[1] + 2 * OWN
    sides = (6, 6, 3, 6, 6, 6, 5)
    planes = (6, 6, 5, 4)
    return pl.pallas_call(
        basis_kernel,
        out_shape=(jax.ShapeDtypeStruct(own, jnp.float32),) * 5
        + (jax.ShapeDtypeStruct((devices, LANES), jnp.float32),),
        in_specs=[SMEM] + [VMEM] * (len(operands) - 1),
        out_specs=(VMEM,) * 6,
        scratch_shapes=[pltpu.VMEM((count, height, LANES), jnp.float32) for count in sides]
        + [pltpu.VMEM((count, 5, height, LANES), jnp.float32) for count in planes],
        compiler_params=params(20),
        name="basis",
    )(*operands)


def product(one, two, moments):
    total = 0.0
    for i, a in enumerate(one):
        for j, b in enumerate(two):
            total = total + a * b * moments[i + j]
    return total


def coefficients(moments, iterations):
    drops = [moments[i] - moments[i + 1] for i in range(MOMENTS - 1)]
    one = jnp.ones_like(moments[0])
    residual, direction, iterate = [one], [one], [0.0 * one] * iterations
    energy = moments[0]
    for iteration in range(iterations):
        step = energy / product(direction, direction, drops)
        iterate = [x + step * (direction[i] if i < len(direction) else 0.0) for i, x in enumerate(iterate)]
        image = [a - b for a, b in zip(direction + [0.0], [0.0] + direction)]
        residual = [a - step * b for a, b in zip(residual + [0.0], image)]
        if iteration + 1 < iterations:
            after = product(residual, residual, moments)
            ratio = after / energy
            direction = [a + ratio * b for a, b in zip(residual, direction + [0.0])]
            energy = after
    return iterate, residual


def update_kernel(
    flag, sums, start, inv, r0_ref, s1_ref, s2_ref, s3_ref, drop_out, residual_out, drop_ref, residual_ref, sems
):
    sums = jnp.sum(sums[...], axis=0, keepdims=True)
    lane = lax.broadcasted_iota(jnp.int32, sums.shape, 1)
    moments = [
        jnp.sum(jnp.where(lane == k, sums, 0.0), axis=1, keepdims=True) for k in range(MOMENTS)
    ]
    x, r = coefficients(moments, 3)
    copies = []
    for k in range(3):
        index = jnp.where(flag[0] == 1, 2 - k, k)
        r0, s1, s2 = r0_ref[k], s1_ref[k], s2_ref[k]
        drop_ref[k] = start[index] + inv[k] * (x[0] * r0 + x[1] * s1 + x[2] * s2)
        residual_ref[k] = r[0] * r0 + r[1] * s1 + r[2] * s2 + r[3] * s3_ref[k]
        copies.append(pltpu.make_async_copy(drop_ref.at[k], drop_out.at[index], sems.at[2 * k]))
        copies.append(pltpu.make_async_copy(residual_ref.at[k], residual_out.at[index], sems.at[2 * k + 1]))
        for copy in copies[-2:]:
            copy.start()
    for copy in copies:
        copy.wait()


def update(*operands):
    own = operands[2].shape
    shape = jax.ShapeDtypeStruct(own, jnp.float32)
    return pl.pallas_call(
        update_kernel,
        out_shape=(shape, shape),
        in_specs=[SMEM] + [VMEM] * (len(operands) - 1),
        out_specs=(HBM, HBM),
        scratch_shapes=[
            pltpu.VMEM(own, jnp.float32),
            pltpu.VMEM(own, jnp.float32),
            pltpu.SemaphoreType.DMA((6,)),
        ],
        compiler_params=params(24),
        name="update",
    )(*operands)


def trade(one, two, axes):
    count = lax.axis_size(axes)
    pairs = [(i, i ^ 1) for i in range(count)]
    shifted = [((i + 1) % count, (j + 1) % count) for i, j in pairs]
    return lax.ppermute(one, axes, pairs), lax.ppermute(two, axes, shifted)


def swap(value):
    return lax.ppermute(value, "layer", [(0, 1), (1, 0)])


def per_device(profiles, time_weight, slot_cell, inst_count, metal, via_density, pad, start_drop):
    rows, cols = metal.shape[1], metal.shape[2]
    gx, gy, layer = lax.axis_index("gx"), lax.axis_index(GY), lax.axis_index("layer")
    flag = jnp.stack(
        [
            layer,
            gx > 0,
            gx < lax.axis_size("gx") - 1,
            gy > 0,
            gy < lax.axis_size(GY) - 1,
            gx % 2,
            gy % 2,
        ]
    ).astype(jnp.int32)
    other_metal = swap(metal)
    other_start = swap(start_drop)
    mine = scatter(profiles, time_weight, slot_cell, inst_count, (rows, cols))
    theirs = swap(mine)
    planes = (flag, metal, other_metal, start_drop, other_start, via_density, pad, mine, theirs)
    edges = [pltpu.VMEM((2, 16, cols), jnp.float32), pltpu.SemaphoreType.DMA((4,))]
    columns = [in_hbm(via_density), in_hbm(pad)]
    strips = strip_call(
        rows_kernel, (64, cols), "rows", flag, *columns, *planes[1:5], far=2, scratch=edges
    )
    strips = strip_call(fed_kernel, (64, cols), "fed", flag, mine, theirs, *strips, in_place=True)
    row_halo = trade(*strips, "gx")
    strips = strip_call(cols_kernel, (rows + 16, LANES), "cols", *planes)
    strips = strip_call(
        corners_kernel, (rows + 16, LANES), "corners", flag, *row_halo, *strips, in_place=True
    )
    col_halo = trade(*strips, GY)
    prepared = links(*planes, *row_halo)
    devices = lax.axis_size(ALL)
    inv, r0, s1, s2, s3, moments = basis(devices, metal.shape, flag, *col_halo, *prepared)
    sums = lax.all_to_all(moments, ALL, 0, 0, tiled=True)
    return update(flag, sums, start_drop, inv, r0, s1, s2, s3)


def solution(mesh):
    split = Mesh(
        mesh.devices.reshape(mesh.shape["gx"], 4, 8, mesh.shape["layer"]),
        ("gx", "gy_0", "gy_1", "layer"),
    )
    grid = P("layer", "gx", GY)
    return jax.shard_map(
        per_device,
        mesh=split,
        in_specs=(P("layer", "gx", GY, None), P(), grid, grid, grid, P("gx", GY), P("gx", GY), grid),
        out_specs=(grid, grid),
        check_vma=False,
    )
```

```python
import jax
import jax.numpy as jnp
from jax import lax
from jax.experimental import pallas as pl
from jax.experimental.pallas import tpu as pltpu
from jax.sharding import Mesh
from jax.sharding import PartitionSpec as P

ALL = ("gx", "gy_0", "gy_1", "layer")
GY = ("gy_0", "gy_1")
HALO = 4
LANES = 128
SIDE = 256
CHUNK = 4096
TINY = 1e-30
MOMENTS = 6

VMEM = pl.BlockSpec(memory_space=pltpu.VMEM)
HBM = pl.BlockSpec(memory_space=pltpu.HBM)
SMEM = pl.BlockSpec(memory_space=pltpu.SMEM)


def params(mebibytes):
    return pltpu.CompilerParams(vmem_limit_bytes=mebibytes << 20)


def scatter_kernel(
    count_ref, weight_hbm, profile_hbm, cell_hbm,
    out_ref, weight_ref, profile_ref, cell_ref, total_ref, sems,
):
    half = out_ref.shape[0]
    blocks = profile_ref.shape[0] // CHUNK
    fetches = [
        pltpu.make_async_copy(cell_hbm, cell_ref, sems.at[blocks]),
        pltpu.make_async_copy(weight_hbm, weight_ref, sems.at[blocks + 1]),
    ]
    for block in range(blocks):
        span = pl.ds(block * CHUNK, CHUNK)
        fetches.append(
            pltpu.make_async_copy(profile_hbm.at[span], profile_ref.at[span], sems.at[block])
        )
    for fetch in fetches:
        fetch.start()
    total_ref[...] = jnp.zeros_like(total_ref)
    ids = lax.broadcasted_iota(jnp.int32, (SIDE, CHUNK), 0).astype(jnp.float32).astype(jnp.bfloat16)
    zero, one = jnp.bfloat16(0), jnp.bfloat16(1)
    fetches[0].wait()
    fetches[1].wait()
    times = weight_ref.shape[0]
    weight = jnp.broadcast_to(weight_ref[...].reshape(1, times), (16, times))

    def add_block(block, _):
        first = pl.multiple_of(block * CHUNK, CHUNK)
        span = pl.ds(first, CHUNK)
        pltpu.make_async_copy(profile_hbm.at[span], profile_ref.at[span], sems.at[block]).wait()
        amount = lax.dot_general(
            weight,
            profile_ref[span, :],
            (((1,), (1,)), ((), ())),
            preferred_element_type=jnp.float32,
        )[:1]
        position = first + lax.broadcasted_iota(jnp.int32, (1, CHUNK), 1)
        amount = jnp.where(position < count_ref[0, 0, 0], amount, 0.0)
        high = amount.astype(jnp.bfloat16)
        low = (amount - high.astype(jnp.float32)).astype(jnp.bfloat16)
        cell = cell_ref[:, span]
        row = ((cell >> 9) + ((cell >> 8) & 1) * half).astype(jnp.float32).astype(jnp.bfloat16)
        col = (cell & (SIDE - 1)).astype(jnp.float32).astype(jnp.bfloat16)
        here = ids == row
        left = jnp.concatenate([jnp.where(here, high, zero), jnp.where(here, low, zero)], axis=0)
        right = jnp.where(ids == col, one, zero)
        total_ref[...] += lax.dot_general(
            left, right, (((1,), (1,)), ((), ())), preferred_element_type=jnp.float32
        )
        return 0

    lax.fori_loop(0, blocks, add_block, 0)
    both = total_ref[:SIDE, :] + total_ref[SIDE:, :]
    out_ref[:, :SIDE] = both[:half]
    out_ref[:, SIDE:] = both[half:]


def in_hbm(value):
    return pltpu.with_memory_space_constraint(value, pltpu.HBM)


def scatter(profiles, time_weight, slot_cell, inst_count, tile):
    slots, times = profiles.shape[-2:]
    return pl.pallas_call(
        scatter_kernel,
        out_shape=jax.ShapeDtypeStruct(tile, jnp.float32),
        in_specs=[SMEM, HBM, HBM, HBM],
        out_specs=VMEM,
        scratch_shapes=[
            pltpu.VMEM((times,), jnp.bfloat16),
            pltpu.VMEM((slots, times), jnp.bfloat16),
            pltpu.VMEM((1, slots), jnp.int32),
            pltpu.VMEM((2 * SIDE, SIDE), jnp.float32),
            pltpu.SemaphoreType.DMA((slots // CHUNK + 2,)),
        ],
        compiler_params=params(20),
        cost_estimate=pl.CostEstimate(
            flops=6 * slots * SIDE * SIDE, bytes_accessed=2 * slots * times, transcendentals=0
        ),
        name="scatter",
    )(
        inst_count,
        in_hbm(time_weight),
        in_hbm(profiles.reshape(slots, times)),
        in_hbm(slot_cell.reshape(1, slots)),
    )


PLANES = 15


class Reader:
    def __init__(self, read, shape):
        self.read, self.shape = read, shape

    def __call__(self, rows, cols):
        return self.read(rows, cols)


def plane_readers(metal, other_metal, start, other_start, via, pad, mine, theirs, flip):
    reads = []
    for own, other in ((metal, other_metal), (start, other_start)):
        for ref in (own, other):
            for k in range(3):
                index = jnp.where(flip == 1, 2 - k, k)
                reads.append(lambda rows, cols, ref=ref, index=index: ref[index, rows, cols])
    if via is not None:
        reads.append(lambda rows, cols: via[rows, cols])
        reads.append(lambda rows, cols: pad[rows, cols])
        reads.append(lambda rows, cols: mine[rows, cols] + theirs[rows, cols])
    return [Reader(read, metal.shape[1:]) for read in reads]


def row_strips(readers, first_plane, flag, one_ref, two_ref):
    rows, cols = readers[0].shape
    low = lax.broadcasted_iota(jnp.int32, (8, cols), 0) < HALO
    for pair in range(0, len(readers), 2):
        packed = []
        for start in (0, rows - 8):
            span = slice(start, start + 8)
            here = readers[pair](span, slice(None))
            there = here
            if pair + 1 < len(readers):
                there = pltpu.roll(readers[pair + 1](span, slice(None)), HALO, 0)
            packed.append(jnp.where(low, here, there) if start == 0 else jnp.where(low, there, here))
        first, last = packed
        start = (first_plane + pair) * HALO
        one_ref[start : start + 8, :] = jnp.where(flag[5] == 1, first, last)
        two_ref[start : start + 8, :] = jnp.where(flag[5] == 1, last, first)


def rows_kernel(flag, via_hbm, pad_hbm, m, om, s, os, one_ref, two_ref, edge_ref, sems):
    rows = m.shape[1]
    fetches = []
    for plane, ref in enumerate((via_hbm, pad_hbm)):
        for side, start in enumerate((0, rows - 8)):
            place = edge_ref.at[plane, pl.ds(8 * side, 8)]
            copy = pltpu.make_async_copy(ref.at[pl.ds(start, 8)], place, sems.at[2 * plane + side])
            copy.start()
            fetches.append(copy)

    def edge(plane):
        return lambda rows, cols: edge_ref[plane, (slice(0, 8) if rows.start == 0 else slice(8, 16)), cols]

    readers = plane_readers(m, om, s, os, None, None, None, None, flag[0])
    row_strips(readers, 0, flag, one_ref, two_ref)
    for fetch in fetches:
        fetch.wait()
    readers = [Reader(edge(plane), m.shape[1:]) for plane in range(2)]
    row_strips(readers, PLANES - 3, flag, one_ref, two_ref)


def fed_kernel(flag, mine, theirs, one_in, two_in, one_ref, two_ref):
    reader = Reader(lambda rows, cols: mine[rows, cols] + theirs[rows, cols], mine.shape)
    done = (PLANES - 1) * HALO
    one_ref[:done, :] = one_in[:done, :]
    two_ref[:done, :] = two_in[:done, :]
    row_strips([reader], PLANES - 1, flag, one_ref, two_ref)


def row_halos(one, two, plane, cols, flag):
    span = slice(plane // 2 * 8, plane // 2 * 8 + 8)
    one, two = one[span, cols], two[span, cols]
    above = jnp.where(flag[1] == 1, jnp.where(flag[5] == 1, one, two), 0.0)
    below = jnp.where(flag[2] == 1, jnp.where(flag[5] == 1, two, one), 0.0)
    if plane % 2:
        return pltpu.roll(above, HALO, 0), pltpu.roll(below, HALO, 0)
    return above, below


def col_strips(values_of, height, cols, flag):
    lane = lax.broadcasted_iota(jnp.int32, (height, LANES), 1)
    sides = []
    for start in (0, cols - LANES):
        span = slice(start, start + LANES)
        packed = jnp.zeros((height, LANES), jnp.float32)
        for plane in range(PLANES):
            values = values_of(plane, span)
            where = HALO * plane if start == 0 else (LANES - HALO + HALO * plane) % LANES
            turned = pltpu.roll(values, HALO * plane, 1) if plane else values
            packed = jnp.where((lane >= where) & (lane < where + HALO), turned, packed)
        sides.append(packed)
    first, last = sides
    return jnp.where(flag[6] == 1, first, last), jnp.where(flag[6] == 1, last, first)


def cols_kernel(flag, m, om, s, os, via, pad, mine, theirs, one_ref, two_ref):
    rows, cols = via.shape
    readers = plane_readers(m, om, s, os, via, pad, mine, theirs, flag[0])
    inner = slice(8, 8 + rows)
    one_ref[inner, :], two_ref[inner, :] = col_strips(
        lambda plane, span: readers[plane](slice(None), span), rows, cols, flag
    )


def corners_kernel(flag, rows_one, rows_two, one_in, two_in, one_ref, two_ref):
    height, cols = one_ref.shape[0], rows_one.shape[1]

    def halos(plane, span):
        return jnp.concatenate(row_halos(rows_one, rows_two, plane, span, flag), axis=0)

    one, two = col_strips(halos, 16, cols, flag)
    for ref, inner, values in ((one_ref, one_in, one), (two_ref, two_in, two)):
        ref[:8, :] = values[:8]
        ref[8 : height - 8, :] = inner[8 : height - 8, :]
        ref[height - 8 :, :] = values[8:]


def col_halo_of(one, two, plane, flag):
    after = jnp.where(flag[6] == 1, two[...], one[...])
    before = jnp.where(flag[6] == 1, one[...], two[...])
    lane = lax.broadcasted_iota(jnp.int32, after.shape, 1)
    where = HALO * plane
    back = (LANES - HALO + where) % LANES
    tail = (lane >= where) & (lane < where + HALO) & (flag[4] == 1)
    head = (lane >= back) & (lane < back + HALO) & (flag[3] == 1)
    values = jnp.where(tail, after, jnp.where(head, before, 0.0))
    return pltpu.roll(values, (LANES - where) % LANES, 1) if plane else values


def strip_call(kernel, shape, name, *operands, far=0, scratch=()):
    last = len(operands) - 1
    return pl.pallas_call(
        kernel,
        out_shape=(jax.ShapeDtypeStruct(shape, jnp.float32),) * 2,
        in_specs=[SMEM] + [HBM] * far + [VMEM] * (last - far),
        out_specs=(VMEM, VMEM),
        scratch_shapes=scratch,
        compiler_params=params(12),
        cost_estimate=pl.CostEstimate(flops=2_000_000, bytes_accessed=1_000_000, transcendentals=0),
        name=name,
    )(*operands)


OWN = 16


def harmonic(values, beside):
    return 2.0 * values * beside / jnp.maximum(values + beside, TINY)


def row_span(i, off=0):
    return pl.ds(OWN + 8 * i + off, 8)


def links_kernel(
    flag, m, om, s, os, via, pad, mine, theirs, rows_one, rows_two,
    row_link, col_link, up_link, total_ref, r_ref, metal_side, start_side,
    metal_ref, start_ref, column_ref,
):
    rows, cols = m.shape[1], m.shape[2]
    tiles, strips = cols // LANES, rows // 8
    readers = plane_readers(m, om, s, os, via, pad, mine, theirs, flag[0])
    places = [(metal_ref, k) for k in range(6)] + [(start_ref, k) for k in range(6)]
    places += [(column_ref, k) for k in range(3)]
    for plane, (read, (ref, k)) in enumerate(zip(readers, places)):
        for j in range(tiles):
            span = slice(j * LANES, j * LANES + LANES)
            above, below = row_halos(rows_one, rows_two, plane, span, flag)
            ref[k, j, OWN - 8 : OWN, :] = above
            ref[k, j, OWN : OWN + rows, :] = read(slice(None), span)
            ref[k, j, OWN + rows : OWN + rows + 8, :] = below

    lane = lax.broadcasted_iota(jnp.int32, (tiles, 8, LANES), 2)
    none = jnp.zeros((1, 8, LANES), jnp.float32)
    weight = jnp.where(flag[0] == 1, 1.0, 0.0)

    def after_col(values):
        turned = pltpu.roll(values, LANES - 1, 2)
        return jnp.where(lane == LANES - 1, jnp.concatenate([turned[1:], none], 0), turned)

    def before_col(values):
        turned = pltpu.roll(values, 1, 2)
        return jnp.where(lane == 0, jnp.concatenate([none, turned[:-1]], 0), turned)

    def body(i, _):
        i = i - 1

        def get(ref, k, off=0):
            return ref[k, :, row_span(i, off), :]

        up, metal, x = None, get(metal_ref, 0), get(start_ref, 0)
        x_before = None
        for k in range(6):
            row = harmonic(metal, get(metal_ref, k, 1))
            row_link[k, :, row_span(i), :] = row
            row_before = get(row_link, k, -1)
            col = harmonic(metal, after_col(metal))
            col_link[k, :, row_span(i), :] = col
            total = row + row_before + col + before_col(col)
            near = row * get(start_ref, k, 1) + row_before * get(start_ref, k, -1)
            near = near + col * after_col(x) + before_col(col * x)
            if k > 0:
                total = total + up
                near = near + up * x_before
            metal_side[k, :, row_span(i), :] = jnp.concatenate([metal[:1], metal[-1:]], 0)
            start_side[k, :, row_span(i), :] = jnp.concatenate([x[:1], x[-1:]], 0)
            x_here = x
            if k < 5:
                metal_after, x = get(metal_ref, k + 1), get(start_ref, k + 1)
                up = get(column_ref, 0) * harmonic(metal, metal_after)
                metal = metal_after
                up_link[k, :, row_span(i), :] = up
                total = total + up
                near = near + up * x
            if k == 0:
                total = total + weight * get(column_ref, 1)
                near = near + (1.0 - weight) * get(column_ref, 2)
            if k == 5:
                total = total + (1.0 - weight) * get(column_ref, 1)
                near = near + weight * get(column_ref, 2)
            total_ref[k, :, row_span(i), :] = total
            r_ref[k, :, row_span(i), :] = near - total * x_here
            x_before = x_here
        return 0

    lax.fori_loop(0, strips + 2, body, 0)


def links(*operands):
    own = operands[1].shape
    counts = [(6, 4), (6, 4), (5, 4), (6, 4), (6, 4), (6, 2), (6, 2)]
    height = own[1] + 2 * OWN
    return pl.pallas_call(
        links_kernel,
        out_shape=[jax.ShapeDtypeStruct(c + (height, LANES), jnp.float32) for c in counts],
        in_specs=[SMEM] + [VMEM] * (len(operands) - 1),
        out_specs=[VMEM] * len(counts),
        scratch_shapes=[pltpu.VMEM((count, 4, height, LANES), jnp.float32) for count in (6, 6, 3)],
        compiler_params=params(28),
        cost_estimate=pl.CostEstimate(flops=80_000_000, bytes_accessed=12_000_000, transcendentals=2_000_000),
        name="links",
    )(*operands)


def basis_kernel(
    flag, cols_one, cols_two, row_link, col_link, up_link, total_ref, r_ref, metal_side, start_side,
    inv_out, r0_out, s1_out, s2_out, s3_out, moments_ref,
    metal_ref, start_ref, column_ref, row_far, col_last, col_far, up_far, inv_ref, z0_ref, z1_ref, z2_ref,
):
    rows, tiles = inv_out.shape[1], col_link.shape[1]
    strips = rows // 8
    inner = slice(OWN - 8, OWN + rows + 8)
    for plane in range(15):
        ref = (metal_ref, start_ref, column_ref)[plane // 6]
        ref[plane % 6, inner, :] = col_halo_of(cols_one, cols_two, plane, flag)

    weight = jnp.where(flag[0] == 1, 1.0, 0.0)
    lane = lax.broadcasted_iota(jnp.int32, (8, LANES), 1)
    zero = jnp.zeros((8, LANES), jnp.float32)

    def later(values):
        return pltpu.roll(values, LANES - 1, values.ndim - 1)

    def earlier(values):
        return pltpu.roll(values, 1, values.ndim - 1)

    def put_own(ref, k, i, values):
        for j in range(tiles):
            ref[k, pl.ds(8 * i, 8), j * LANES : j * LANES + LANES] = values[j]

    def fold(values):
        return jnp.sum(values[:tiles], axis=0)

    def sweep(body, count):
        body(-1, None)
        sums = lax.fori_loop(0, strips, body, (zero,) * count)
        body(strips, None)
        return sums

    def first(i, sums):
        def get(ref, k, off=0):
            return ref[k, row_span(i, off), :]

        energy = None if sums is None else sums[0]
        up = None
        for k in range(6):
            metal, x = get(metal_ref, k), get(start_ref, k)
            metal_first, metal_last = metal_side[k, 0, row_span(i), :], metal_side[k, 1, row_span(i), :]
            x_first, x_last = start_side[k, 0, row_span(i), :], start_side[k, 1, row_span(i), :]
            row = harmonic(metal, get(metal_ref, k, 1))
            row_far[k, row_span(i), :] = row
            row_before = get(row_far, k, -1)
            metal_later = later(metal)
            last = jnp.where(lane == LANES - 1, harmonic(metal_last, metal_later), 0.0)
            col_last[k, row_span(i), :] = col_link[k, tiles - 1, row_span(i), :] + last
            col = harmonic(metal, jnp.where(lane == LANES - 1, later(metal_first), metal_later))
            col_far[k, row_span(i), :] = col
            col_earlier, x_later = earlier(col), later(x)
            total = row + row_before + col + jnp.where(lane == 0, earlier(last), col_earlier)
            near = row * get(start_ref, k, 1) + row_before * get(start_ref, k, -1)
            near = near + col * jnp.where(lane == LANES - 1, later(x_first), x_later)
            near = near + jnp.where(lane == 0, earlier(last * x_last), earlier(col * x))
            if k > 0:
                total = total + up
                near = near + up * get(start_ref, k - 1)
            if k < 5:
                up = get(column_ref, 0) * harmonic(metal, get(metal_ref, k + 1))
                up_far[k, row_span(i), :] = up
                total = total + up
                near = near + up * get(start_ref, k + 1)
            if k == 0:
                total = total + weight * get(column_ref, 1)
                near = near + (1.0 - weight) * get(column_ref, 2)
            if k == 5:
                total = total + (1.0 - weight) * get(column_ref, 1)
                near = near + weight * get(column_ref, 2)
            before = jnp.where(lane == 0, col_earlier, 0.0)
            totals, r = total_ref[k, :, row_span(i), :], r_ref[k, :, row_span(i), :]
            totals = [totals[0] + before, totals[1], totals[2], totals[3] + last, total]
            r = [
                r[0] + before * (earlier(x) - x_first),
                r[1],
                r[2],
                r[3] + last * (x_later - x_last),
                near - total * x,
            ]
            inv, r = 1.0 / jnp.maximum(jnp.stack(totals), TINY), jnp.stack(r)
            z = r * inv
            inv_ref[k, :, row_span(i), :] = inv
            z0_ref[k, :, row_span(i), :] = z
            if sums is not None and k < 3:
                put_own(inv_out, k, i, inv)
                put_own(r0_out, k, i, r)
                energy = energy + fold(z * r)
        return None if sums is None else (energy,)

    def step(source, target, out, planes):
        width = tiles if target is None else tiles + 1
        ends = lax.broadcasted_iota(jnp.int32, (width, 8, LANES), 2)

        def body(i, sums):
            def get(k, off=0):
                return source[k, :width, row_span(i, off), :]

            def whole(near_ref, far_ref, k, off=0):
                near = near_ref[k, :, row_span(i, off), :]
                if width == tiles:
                    return near
                return jnp.concatenate([near, far_ref[k, row_span(i, off), :][None]], 0)

            totals = sums
            up, z_before = None, None
            z = source[0, :, row_span(i), :]
            for k in range(planes):
                col = jnp.concatenate(
                    [
                        col_link[k, : tiles - 1, row_span(i), :],
                        col_last[k, row_span(i), :][None],
                        col_far[k, row_span(i), :][None],
                    ],
                    0,
                )
                turned = later(z)
                following = jnp.concatenate([turned[1:], turned[:1]], 0)
                z_later = jnp.where(ends == LANES - 1, following[:width], turned[:width])
                turned = earlier(col * z)
                preceding = jnp.concatenate([turned[-1:], turned[:-1]], 0)
                near = col[:width] * z_later + jnp.where(ends == 0, preceding[:width], turned[:width])
                near = near + whole(row_link, row_far, k) * get(k, 1)
                near = near + whole(row_link, row_far, k, -1) * get(k, -1)
                if k > 0:
                    near = near + up * z_before
                z_after = source[k + 1, :, row_span(i), :]
                up = whole(up_link, up_far, k) if k < 5 else None
                if k < 5:
                    near = near + up * z_after[:width]
                z_here = z[:width]
                if target is not None:
                    fresh = near * inv_ref[k, :, row_span(i), :]
                    target[k, :, row_span(i), :] = fresh
                if sums is not None and k < 3:
                    put_own(out, k, i, near)
                    terms = (z_here * near,) if target is None else (z_here * near, fresh * near)
                    totals = tuple(a + fold(b) for a, b in zip(totals, terms))
                z_before, z = z_here, z_after
            return totals

        return body

    sums = sweep(first, 1)
    sums += sweep(step(z0_ref, z1_ref, s1_out, 5), 2)
    sums += sweep(step(z1_ref, z2_ref, s2_out, 4), 2)
    sums += lax.fori_loop(0, strips, step(z2_ref, None, s3_out, 3), (zero,))
    packed = zero
    for k, total in enumerate(sums):
        packed = jnp.where(lane == k, jnp.sum(total, keepdims=True), packed)
    moments_ref[...] = jnp.broadcast_to(packed[:1], moments_ref.shape)


def basis(devices, own, *operands):
    height = own[1] + 2 * OWN
    sides = (6, 6, 3, 6, 6, 6, 5)
    planes = (6, 6, 5, 4)
    return pl.pallas_call(
        basis_kernel,
        out_shape=(jax.ShapeDtypeStruct(own, jnp.float32),) * 5
        + (jax.ShapeDtypeStruct((devices, LANES), jnp.float32),),
        in_specs=[SMEM] + [VMEM] * (len(operands) - 1),
        out_specs=(VMEM,) * 6,
        scratch_shapes=[pltpu.VMEM((count, height, LANES), jnp.float32) for count in sides]
        + [pltpu.VMEM((count, 5, height, LANES), jnp.float32) for count in planes],
        compiler_params=params(36),
        name="basis",
    )(*operands)


def product(one, two, moments):
    total = 0.0
    for i, a in enumerate(one):
        for j, b in enumerate(two):
            total = total + a * b * moments[i + j]
    return total


def coefficients(moments, iterations):
    drops = [moments[i] - moments[i + 1] for i in range(MOMENTS - 1)]
    one = jnp.ones_like(moments[0])
    residual, direction, iterate = [one], [one], [0.0 * one] * iterations
    energy = moments[0]
    for iteration in range(iterations):
        step = energy / product(direction, direction, drops)
        iterate = [x + step * (direction[i] if i < len(direction) else 0.0) for i, x in enumerate(iterate)]
        image = [a - b for a, b in zip(direction + [0.0], [0.0] + direction)]
        residual = [a - step * b for a, b in zip(residual + [0.0], image)]
        if iteration + 1 < iterations:
            after = product(residual, residual, moments)
            ratio = after / energy
            direction = [a + ratio * b for a, b in zip(residual, direction + [0.0])]
            energy = after
    return iterate, residual


def update_kernel(
    flag, sums, start, inv, r0_ref, s1_ref, s2_ref, s3_ref, drop_out, residual_out, drop_ref, residual_ref, sems
):
    sums = jnp.sum(sums[...], axis=0, keepdims=True)
    lane = lax.broadcasted_iota(jnp.int32, sums.shape, 1)
    moments = [
        jnp.sum(jnp.where(lane == k, sums, 0.0), axis=1, keepdims=True) for k in range(MOMENTS)
    ]
    x, r = coefficients(moments, 3)
    copies = []
    for k in range(3):
        index = jnp.where(flag[0] == 1, 2 - k, k)
        r0, s1, s2 = r0_ref[k], s1_ref[k], s2_ref[k]
        drop_ref[k] = start[index] + inv[k] * (x[0] * r0 + x[1] * s1 + x[2] * s2)
        residual_ref[k] = r[0] * r0 + r[1] * s1 + r[2] * s2 + r[3] * s3_ref[k]
        copies.append(pltpu.make_async_copy(drop_ref.at[k], drop_out.at[index], sems.at[2 * k]))
        copies.append(pltpu.make_async_copy(residual_ref.at[k], residual_out.at[index], sems.at[2 * k + 1]))
        for copy in copies[-2:]:
            copy.start()
    for copy in copies:
        copy.wait()


def update(*operands):
    own = operands[2].shape
    shape = jax.ShapeDtypeStruct(own, jnp.float32)
    return pl.pallas_call(
        update_kernel,
        out_shape=(shape, shape),
        in_specs=[SMEM] + [VMEM] * (len(operands) - 1),
        out_specs=(HBM, HBM),
        scratch_shapes=[
            pltpu.VMEM(own, jnp.float32),
            pltpu.VMEM(own, jnp.float32),
            pltpu.SemaphoreType.DMA((6,)),
        ],
        compiler_params=params(24),
        name="update",
    )(*operands)


def trade(one, two, axes):
    count = lax.axis_size(axes)
    pairs = [(i, i ^ 1) for i in range(count)]
    shifted = [((i + 1) % count, (j + 1) % count) for i, j in pairs]
    return lax.ppermute(one, axes, pairs), lax.ppermute(two, axes, shifted)


def swap(value):
    return lax.ppermute(value, "layer", [(0, 1), (1, 0)])


def per_device(profiles, time_weight, slot_cell, inst_count, metal, via_density, pad, start_drop):
    rows, cols = metal.shape[1], metal.shape[2]
    gx, gy, layer = lax.axis_index("gx"), lax.axis_index(GY), lax.axis_index("layer")
    flag = jnp.stack(
        [
            layer,
            gx > 0,
            gx < lax.axis_size("gx") - 1,
            gy > 0,
            gy < lax.axis_size(GY) - 1,
            gx % 2,
            gy % 2,
        ]
    ).astype(jnp.int32)
    other_metal = swap(metal)
    other_start = swap(start_drop)
    mine = scatter(profiles, time_weight, slot_cell, inst_count, (rows, cols))
    theirs = swap(mine)
    planes = (flag, metal, other_metal, start_drop, other_start, via_density, pad, mine, theirs)
    edges = [pltpu.VMEM((2, 16, cols), jnp.float32), pltpu.SemaphoreType.DMA((4,))]
    columns = [in_hbm(via_density), in_hbm(pad)]
    strips = strip_call(
        rows_kernel, (64, cols), "rows", flag, *columns, *planes[1:5], far=2, scratch=edges
    )
    strips = strip_call(fed_kernel, (64, cols), "fed", flag, mine, theirs, *strips)
    row_halo = trade(*strips, "gx")
    strips = strip_call(cols_kernel, (rows + 16, LANES), "cols", *planes)
    strips = strip_call(
        corners_kernel, (rows + 16, LANES), "corners", flag, *row_halo, *strips
    )
    col_halo = trade(*strips, GY)
    prepared = links(*planes, *row_halo)
    devices = lax.axis_size(ALL)
    inv, r0, s1, s2, s3, moments = basis(devices, metal.shape, flag, *col_halo, *prepared)
    sums = lax.all_to_all(moments, ALL, 0, 0, tiled=True)
    return update(flag, sums, start_drop, inv, r0, s1, s2, s3)


def solution(mesh):
    split = Mesh(
        mesh.devices.reshape(mesh.shape["gx"], 4, 8, mesh.shape["layer"]),
        ("gx", "gy_0", "gy_1", "layer"),
    )
    grid = P("layer", "gx", GY)
    return jax.shard_map(
        per_device,
        mesh=split,
        in_specs=(P("layer", "gx", GY, None), P(), grid, grid, grid, P("gx", GY), P("gx", GY), grid),
        out_specs=(grid, grid),
        check_vma=False,
    )
```
